256 devices in a mesh: tm: 16 (over y_hi, z), batch: 8 (over x, core), width: 2 (over y_lo).
Axes of the slice: x: 4, y: 4 (y_hi: 2, y_lo: 2; y = y_hi * 2 + y_lo), z: 8, core: 2. Of those that a mesh axis runs over, the one named last changes fastest.
Arguments:
- moves: int32 [16, 4096], P('batch', 'tm'), may hold values from 0 to 361
- lengths: int32 [16], P('batch'), may hold values from 1 to 4096
- outcomes: int32 [16], P('batch'), may hold values from -1 to 1
- embedded: bfloat16 [16, 4096, 2048], P('batch', 'tm', 'width'), may hold values from -6 to 6
- w_branches: bfloat16 [4, 2048, 2048], P(None, ('tm', 'batch'), 'width'), may hold values from -0.125 to 0.125
- conv_w: float32 [4, 2048], P(None, 'width'), may hold values from -3 to 3
- gate_bias: float32 [2, 2048], P(None, 'width'), may hold values from -4 to 4
- rates: float32 [2048], P('width'), may hold values from 0.001 to 0.105
- w_down: bfloat16 [2048, 2048], P(('tm', 'batch'), 'width'), may hold values from -0.125 to 0.125
- w_policy: bfloat16 [2048, 362], P('width'), may hold values from -12 to 12
- w_value: bfloat16 [2048], P('width'), may hold values from -0.125 to 0.125
Outputs:
- position_loss: float32 [16, 4096], P('batch', 'tm')
- value: float32 [16, 4096], P('batch', 'tm')
The draws below stay inside these ranges and needn't reach their ends.
All inputs are finite; a program needn't handle non-finite values.
Results may differ from the reference program's by a relative error of at most 0.0033.
Values may be sent and summed in bfloat16 or wider, within the bound.
No kernel may reach another device: no remote copies, remote signals or barrier semaphores. Data moves between devices by JAX's collectives and lax.ppermute only.
A program may use at most 128 MiB of HBM per device.

```python
import math
import jax
import jax.numpy as jnp
from jax import lax

D = 2048
R = 2048
MOVES = 362
KERNEL = 4
GAMES = 16
TIME = 4096


def draw_w_policy(key, part):
    first = jax.random.fold_in(jax.random.fold_in(key, 17), 0)
    base = jax.random.normal(first, (D, MOVES), jnp.float32) / math.sqrt(D)
    return jnp.clip(base, -12.0, 12.0).astype(jnp.bfloat16)


def set_ends(values, rng, least, largest):
    longest = values.shape.index(max(values.shape))
    spots = []
    for shift in (0, 1):
        where = [jax.random.randint(jax.random.fold_in(rng, axis), (), 0, length) for axis, length in enumerate(values.shape)]
        where[longest] = (where[longest] + shift) % values.shape[longest]
        spots.append(tuple(where))
    return values.at[spots[0]].set(least).at[spots[1]].set(largest)


def shard_levels(rng, dims, cuts, least, top_value):
    def one(axis_at, shards_of):
        steps = jax.random.uniform(jax.random.fold_in(jax.random.fold_in(rng, 6), axis_at), (shards_of,), jnp.float32, least / len(cuts), top_value / len(cuts))
        return jnp.repeat(jnp.exp(steps), dims[axis_at] // shards_of).reshape((-1,) + (1,) * (len(dims) - axis_at - 1))

    level = one(*cuts[0])
    for cut in cuts[1:]:
        level = level * one(*cut)
    return level


def gaussian(stream_key, extent, deviation, reach, cuts=(), kind=jnp.bfloat16):
    level = shard_levels(stream_key, extent, cuts, -0.22, 0.18) if cuts else 1.0
    entries = jax.random.normal(stream_key, extent, jnp.float32) * deviation * level
    return jnp.minimum(jnp.maximum(entries, -reach), reach).astype(kind)


def setup_inputs(seed: int = 0) -> dict:
    key_list = jax.random.split(jax.random.key(seed), 12)
    moves = set_ends(jax.random.randint(key_list[0], (GAMES, TIME), 0, MOVES), jax.random.fold_in(key_list[0], 1), 0, MOVES - 1).astype(jnp.int32)
    lengths = set_ends(jax.random.randint(key_list[1], (GAMES,), 1, TIME + 1), jax.random.fold_in(key_list[1], 1), 1, TIME).astype(jnp.int32)
    outcomes = set_ends(jax.random.randint(key_list[2], (GAMES,), -1, 2), jax.random.fold_in(key_list[2], 1), -1, 1).astype(jnp.int32)
    embedded = gaussian(key_list[3], (GAMES, TIME, D), 1.0, 6.0, ((0, 8), (1, 16), (2, 2)))
    w_branches = gaussian(key_list[4], (4, D, R), D ** -0.5, 0.125, ((1, 128), (2, 2)))
    conv_w = gaussian(key_list[5], (KERNEL, R), 0.5, 3.0, ((1, 2),), jnp.float32)
    gate_bias = gaussian(key_list[6], (2, R), 1.0, 4.0, ((1, 2),), jnp.float32)
    rates = jnp.clip(jnp.exp(math.log(0.105) - 4.65396 * jax.random.uniform(key_list[7], (R,), jnp.float32) ** shard_levels(key_list[7], (R,), ((0, 2),), -0.2, 0.2)), 0.001, 0.105)
    w_down = gaussian(key_list[8], (D, R), R ** -0.5, 0.125, ((0, 128), (1, 2)))
    w_policy = draw_w_policy(jax.random.fold_in(key_list[11], 71), 0)
    w_value = gaussian(key_list[10], (D,), D ** -0.5, 0.125, ((0, 2),))
    return {"moves": moves, "lengths": lengths, "outcomes": outcomes, "embedded": embedded, "w_branches": w_branches, "conv_w": conv_w, "gate_bias": gate_bias, "rates": rates, "w_down": w_down, "w_policy": w_policy, "w_value": w_value}


def link(early, late):
    return (early[0] + late[0], jnp.exp(late[0]) * early[1] + late[1])

def reference(moves, lengths, outcomes, embedded, w_branches, conv_w, gate_bias, rates, w_down, w_policy, w_value):

    def one_game(packed):
        feats, played, length, result = packed
        proj = [jnp.dot(feats, w_branches[k], preferred_element_type=jnp.float32) for k in range(4)]
        gated = jax.nn.gelu(proj[0])
        padded = jnp.concatenate([jnp.zeros((KERNEL - 1, R), jnp.float32), proj[1]], 0)
        conv = jnp.zeros((TIME, R), jnp.float32)
        for k in range(KERNEL):
            conv = conv + conv_w[k] * padded[KERNEL - 1 - k:KERNEL - 1 - k + TIME]
        recur = jax.nn.sigmoid(proj[2] + gate_bias[0])
        inflow = jax.nn.sigmoid(proj[3] + gate_bias[1])
        log_a = -8.0 * recur * rates
        decay = jnp.exp(log_a)
        drive = jnp.sqrt(1.0 - decay * decay) * inflow * conv
        summed, hidden = lax.associative_scan(link, (log_a, drive), axis=0)
        mixed = (hidden * gated).astype(jnp.bfloat16)
        down = lax.dot_general(mixed, w_down, (((1,), (1,)), ((), ())), preferred_element_type=jnp.float32)
        resid = (feats.astype(jnp.float32) + down).astype(jnp.bfloat16)
        wide = resid.astype(jnp.float32)
        sumsq = lax.optimization_barrier(jnp.sum(wide * wide, -1))
        norm = lax.rsqrt(sumsq / D + 1e-06)
        logits = jnp.dot(resid, w_policy, preferred_element_type=jnp.float32) * norm[:, None]
        value = jnp.tanh(jnp.dot(resid, w_value, preferred_element_type=jnp.float32) * norm)
        top = lax.optimization_barrier(jnp.max(logits, -1, keepdims=True))
        lse = top[:, 0] + jnp.log(lax.optimization_barrier(jnp.sum(jnp.exp(logits - top), -1)))
        column = lax.broadcasted_iota(jnp.int32, (TIME, MOVES), 1)
        picked = lax.optimization_barrier(jnp.sum(jnp.where(column == played[:, None], logits, 0.0), -1))
        target = result.astype(jnp.float32)
        where_live = jnp.arange(TIME, dtype=jnp.int32) < length
        loss = jnp.where(where_live, lse - picked + (value - target) ** 2, 0.0)
        return (loss, value)
    return lax.map(one_game, (embedded, moves, lengths, outcomes))
```

```python
import jax
import jax.numpy as jnp
from jax import lax
from jax.experimental import pallas as pl
from jax.experimental.pallas import tpu as pltpu
from jax.sharding import Mesh
from jax.sharding import PartitionSpec as P

D = 2048
HALF = 1024
KERNEL = 4
MOVES = 362
COLS = 384
STEPS = 256
CH = 256
SEQS = 8
LANES = CH // 128
TAIL = 8
VMEM_LIMIT = 56 * 1024 * 1024

F32 = jnp.float32
BF16 = jnp.bfloat16
ANY = pl.BlockSpec(memory_space=pl.ANY)
VM = pl.BlockSpec(memory_space=pltpu.VMEM)
SM = pl.BlockSpec(memory_space=pltpu.SMEM)

PAIR = [(0, 1), (1, 0), (2, 3), (3, 2)]
OTHER = [(0, 3), (3, 0), (1, 2), (2, 1)]
SWAP = [(0, 1), (1, 0)]


def dot(a, b):
    return jnp.dot(a, b, preferred_element_type=F32)


def piece_copies(pieces, xa, xb, sems):
    copies = []
    for core, (own, pair, other, far0, far1) in enumerate(pieces):
        first = pl.ds(core * 2, 2)
        second = pl.ds(4 + core * 2, 2)
        k = core * 5
        copies.append(pltpu.make_async_copy(own, xa.at[first], sems.at[k]))
        copies.append(pltpu.make_async_copy(pair, xb.at[first], sems.at[k + 1]))
        copies.append(pltpu.make_async_copy(far0, xa.at[4 + core * 2], sems.at[k + 2]))
        copies.append(pltpu.make_async_copy(far1, xa.at[5 + core * 2], sems.at[k + 3]))
        copies.append(pltpu.make_async_copy(other, xb.at[second], sems.at[k + 4]))
    return copies


def weight_copies(gathered, held, sems):
    copies = []
    for b in range(held.shape[0]):
        for h in range(2):
            copies.append(
                pltpu.make_async_copy(gathered.at[:, b, h], held.at[b, h], sems.at[b * 2 + h])
            )
    return copies


def half_of(held, branch, half):
    return held[branch, half].reshape(HALF, CH)


def recur_kernel(meta, *refs):
    pieces = (refs[0:5], refs[5:10])
    gathered, tail_a, tail_b, conv_w, bias, rates = refs[10:16]
    decays, states, ends = refs[16:19]
    xa, xb, held, ext, tails, x_sems, w_sems = refs[19:]
    w = meta[0]
    to_held = weight_copies(gathered, held, w_sems)
    to_x = piece_copies(pieces, xa, xb, x_sems)
    for copy in to_held:
        copy.start()
    for copy in to_x:
        copy.start()
    for copy in to_held:
        copy.wait()
    for copy in to_x:
        copy.wait()
    tails[...] = dot(tail_a[...], half_of(held, 0, w)) + dot(tail_b[...], half_of(held, 0, 1 - w))

    def one(i, carry):
        a, b = xa[i], xb[i]

        def proj(branch):
            return dot(a, half_of(held, branch, w)) + dot(b, half_of(held, branch, 1 - w))

        source = proj(0)
        ext[0:TAIL] = tails[pl.ds(pl.multiple_of(i * TAIL, TAIL), TAIL)]
        ext[TAIL:] = source
        conv = conv_w[0:1] * source
        for k in range(1, KERNEL):
            conv = conv + conv_w[k : k + 1] * ext[TAIL - k : TAIL - k + STEPS]
        recur = jax.nn.sigmoid(proj(1) + bias[0:1])
        inflow = jax.nn.sigmoid(proj(2) + bias[1:2])
        decay = jnp.exp(-8.0 * recur * rates[...])
        drive = jnp.sqrt(1.0 - decay * decay) * inflow * conv
        for lane in range(LANES):
            cols = slice(lane * 128, (lane + 1) * 128)
            decays[lane, pl.ds(i, STEPS, stride=SEQS), :] = decay[:, cols]
            states[lane, pl.ds(i, STEPS, stride=SEQS), :] = drive[:, cols]
        return carry

    lax.fori_loop(0, SEQS, one, 0)

    def step(t, carry):
        at = pl.ds(pl.multiple_of(t * SEQS, SEQS), SEQS)
        done = []
        for lane, (state, product) in enumerate(carry):
            decay = decays[lane, at]
            state = decay * state + states[lane, at]
            product = product * decay
            states[lane, at] = state
            decays[lane, at] = product
            done.append((state, product))
        return tuple(done)

    start = (jnp.zeros((SEQS, 128), F32), jnp.ones((SEQS, 128), F32))
    last = lax.fori_loop(0, STEPS, step, (start,) * LANES, unroll=8)
    for lane, (state, product) in enumerate(last):
        ends[0, :, lane * 128 : (lane + 1) * 128] = product
        ends[1, :, lane * 128 : (lane + 1) * 128] = state


def gate_kernel(meta, *refs):
    pieces = (refs[0:5], refs[5:10])
    gathered, gated = refs[10:12]
    xa, xb, held, x_sems, w_sems = refs[12:]
    w = meta[0]
    to_held = weight_copies(gathered, held, w_sems)
    to_x = piece_copies(pieces, xa, xb, x_sems)
    for copy in to_held:
        copy.start()
    for copy in to_x:
        copy.start()
    for copy in to_held:
        copy.wait()
    for copy in to_x:
        copy.wait()

    def one(i, carry):
        proj = dot(xa[i], half_of(held, 0, w)) + dot(xb[i], half_of(held, 0, 1 - w))
        gated[i] = jax.nn.gelu(proj)
        return carry

    lax.fori_loop(0, SEQS, one, 0)


def mix_kernel(meta, decays, states, gated, blocks, mixed):
    c, yh, z = meta[1], meta[2], meta[3]
    row = lax.broadcasted_iota(jnp.int32, (SEQS, CH), 0)
    late = jnp.where(row < 4, yh, 1 - yh) == 1
    whole = jnp.zeros((SEQS, CH), F32)
    for k in range(8):
        whole = blocks[k, 0] * whole + blocks[k, 1]
    incoming = jnp.where(late, pltpu.roll(whole, 4, 0), 0.0)
    for k in range(8):
        incoming = jnp.where(k < z, blocks[k, 0] * incoming + blocks[k, 1], incoming)
    for i in range(SEQS):
        block, core, game = i // 4, (i // 2) % 2, i % 2
        at = pl.ds(i, STEPS, stride=SEQS)
        yb = yh if block == 0 else 1 - yh
        cb = c if core == 0 else 1 - c
        target = (yb * 2 + cb) * 2 + game
        for lane in range(LANES):
            cols = slice(lane * 128, (lane + 1) * 128)
            hidden = states[lane, at, :] + decays[lane, at, :] * incoming[i : i + 1, cols]
            mixed[target, :, cols] = (hidden * gated[i, :, cols]).astype(BF16)


def head_kernel(
    meta, own, pair, mixed, wd_own, wd_oth, wp_own, wp_oth, moves, out, feat, down_w, resid, sems
):
    w, c, tm, length, outcome = meta[0], meta[1], meta[4], meta[5], meta[6]
    copies = [
        pltpu.make_async_copy(own.at[w], feat.at[w], sems.at[0]),
        pltpu.make_async_copy(pair.at[w], feat.at[1 - w], sems.at[1]),
    ]
    for k, (src, core) in enumerate(((wd_own, c), (wd_oth, 1 - c))):
        for h in range(2):
            for v in range(2):
                copies.append(
                    pltpu.make_async_copy(
                        src.at[:, h * 2 + v],
                        down_w.at[h, :, core, :, pl.ds(v * HALF, HALF)],
                        sems.at[2 + k * 4 + h * 2 + v],
                    )
                )
    for copy in copies:
        copy.start()
    order = [(h * 2 + k) * 2 + v for v in range(2) for h in range(2) for k in range(2)]
    mix = jnp.concatenate([mixed[j] for j in order], axis=1)
    for copy in copies:
        copy.wait()
    square = jnp.zeros((STEPS, 1), F32)
    width = 512
    for h in range(2):
        for j in range(2):
            rows = down_w[h, j * 16 : (j + 1) * 16].reshape(width, D)
            down = lax.dot_general(
                mix, rows, (((1,), (1,)), ((), ())), preferred_element_type=F32
            )
            at = slice(j * width, (j + 1) * width)
            value = (feat[h, :, at].astype(F32) + down).astype(BF16)
            resid[h, :, at] = value
            wide = value.astype(F32)
            square = square + jnp.sum(wide * wide, axis=1, keepdims=True)
    raw = dot(resid[w], wp_own[...]) + dot(resid[1 - w], wp_oth[...])
    norm = lax.rsqrt(square / D + 1e-06)
    logits = raw * norm
    column = lax.broadcasted_iota(jnp.int32, logits.shape, 1)
    policy = column < MOVES
    top = jnp.max(jnp.where(policy, logits, -jnp.inf), axis=1, keepdims=True)
    total = jnp.sum(jnp.where(policy, jnp.exp(logits - top), 0.0), axis=1, keepdims=True)
    lse = top + jnp.log(total)
    picked = jnp.sum(jnp.where(column == moves[...], logits, 0.0), axis=1, keepdims=True)
    score = jnp.sum(jnp.where(column == MOVES, logits, 0.0), axis=1, keepdims=True)
    value = jnp.tanh(score)
    place = tm * STEPS + lax.broadcasted_iota(jnp.int32, (STEPS, 1), 0)
    loss = jnp.where(place < length, lse - picked + (value - outcome.astype(F32)) ** 2, 0.0)
    lane = lax.broadcasted_iota(jnp.int32, (STEPS, 128), 1)
    both = jnp.where(lane == 0, loss, jnp.where(lane == 1, value, 0.0))
    out[...] = both.T[0:8]


def params():
    return pltpu.CompilerParams(vmem_limit_bytes=VMEM_LIMIT)


def sent_to_all(x, axis):
    length = lax.axis_size(axis)
    return lax.all_to_all(jnp.broadcast_to(x[None], (length, *x.shape)), axis, 0, 0, tiled=True)


def shards(
    moves,
    lengths,
    outcomes,
    embedded,
    w_branches,
    conv_w,
    gate_bias,
    rates,
    w_down,
    w_policy,
    w_value,
):
    yh, z, c, w = (lax.axis_index(a) for a in ("yh", "z", "c", "w"))
    tm = yh * 8 + z
    sel = lambda a: lax.dynamic_index_in_dim(a, w, 0, keepdims=False)
    meta = jnp.stack([w, c, yh, z, tm, sel(lengths), sel(outcomes)]).astype(jnp.int32)

    quarters = w_branches.reshape(4, 16, 4, CH).transpose(2, 0, 1, 3)
    quarters = lax.all_to_all(quarters, ("yh", "c"), 0, 0, tiled=True)
    shard = quarters.reshape(2, 2, 4, 16, CH).transpose(2, 0, 1, 3, 4).reshape(4, 2, 32, CH)
    w_recur = lax.all_gather(shard[1:], ("z", "x"), axis=0)
    w_gate = lax.all_gather(shard[:1], ("z", "x"), axis=0)
    downs = sent_to_all(w_down, ("yh", "w"))
    wd_own = lax.all_gather(downs, ("z", "x"), axis=0)
    wd_oth = lax.ppermute(wd_own, "c", SWAP)

    ring = ("yh", "w")
    own = embedded
    pair = lax.ppermute(own, ring, PAIR)
    other = lax.ppermute(own, ring, OTHER)
    far0 = lax.ppermute(other[0], ring, PAIR)
    far1 = lax.ppermute(pair[1], ring, OTHER)
    mine = (own, pair, other, far0, far1)
    theirs = tuple(lax.ppermute(p, "c", SWAP) for p in mine)

    tail_a = jnp.concatenate(
        [a.reshape(-1, STEPS, HALF)[:, STEPS - TAIL :] for a in (mine[0], theirs[0], mine[3], mine[4], theirs[3], theirs[4])]
    )
    tail_b = jnp.concatenate(
        [a[:, STEPS - TAIL :] for a in (mine[1], theirs[1], mine[2], theirs[2])]
    )
    tail = lax.ppermute(
        jnp.stack([tail_a, tail_b]).reshape(2, 2, 4 * TAIL, HALF), "z", [(k, (k + 1) % 8) for k in range(8)]
    )
    late = jnp.stack([yh, 1 - yh]).reshape(1, 2, 1, 1) == 1
    tail = jnp.where(z > 0, tail, jnp.where(late, tail[:, ::-1], jnp.zeros_like(tail)))
    tail = tail.reshape(2, SEQS * TAIL, HALF)

    q = (yh * 2 + c) * CH
    cut = lambda a: lax.dynamic_slice_in_dim(a, q, CH, a.ndim - 1)
    x_scratch = [
        pltpu.VMEM((SEQS, STEPS, HALF), BF16),
        pltpu.VMEM((SEQS, STEPS, HALF), BF16),
    ]
    decays, states, ends = pl.pallas_call(
        recur_kernel,
        name="recur",
        out_shape=(
            jax.ShapeDtypeStruct((LANES, STEPS * SEQS, 128), F32),
            jax.ShapeDtypeStruct((LANES, STEPS * SEQS, 128), F32),
            jax.ShapeDtypeStruct((2, SEQS, CH), F32),
        ),
        in_specs=[SM] + [ANY] * 11 + [VM] * 5,
        out_specs=(VM, VM, VM),
        scratch_shapes=x_scratch
        + [
            pltpu.VMEM((3, 2, 32, 32, CH), BF16),
            pltpu.VMEM((TAIL + STEPS, CH), F32),
            pltpu.VMEM((SEQS * TAIL, CH), F32),
            pltpu.SemaphoreType.DMA((10,)),
            pltpu.SemaphoreType.DMA((6,)),
        ],
        compiler_params=params(),
        cost_estimate=pl.CostEstimate(
            flops=2 * 2048 * 2048 * 768, bytes_accessed=15 << 20, transcendentals=5 << 19
        ),
    )(meta, *mine, *theirs, w_recur, tail[0], tail[1], cut(conv_w), cut(gate_bias), cut(rates[None]))

    blocks = sent_to_all(ends, "z")
    gated = pl.pallas_call(
        gate_kernel,
        name="gate",
        out_shape=jax.ShapeDtypeStruct((SEQS, STEPS, CH), F32),
        in_specs=[SM] + [ANY] * 11,
        out_specs=VM,
        scratch_shapes=x_scratch
        + [
            pltpu.VMEM((1, 2, 32, 32, CH), BF16),
            pltpu.SemaphoreType.DMA((10,)),
            pltpu.SemaphoreType.DMA((2,)),
        ],
        compiler_params=params(),
        cost_estimate=pl.CostEstimate(
            flops=2 * 2048 * 2048 * 256, bytes_accessed=11 << 20, transcendentals=1 << 19
        ),
    )(meta, *mine, *theirs, w_gate)

    mixed = pl.pallas_call(
        mix_kernel,
        name="mix",
        out_shape=jax.ShapeDtypeStruct((SEQS, STEPS, CH), BF16),
        in_specs=[SM] + [VM] * 4,
        out_specs=VM,
        compiler_params=params(),
        cost_estimate=pl.CostEstimate(flops=4 << 19, bytes_accessed=7 << 20, transcendentals=0),
    )(meta, decays, states, gated, blocks)
    mixed = lax.all_to_all(mixed, ("yh", "c", "w"), 0, 0, tiled=True)

    heads = jnp.concatenate(
        [w_policy, w_value[:, None], jnp.zeros((HALF, COLS - MOVES - 1), BF16)], axis=1
    )
    heads_oth = lax.ppermute(heads, "w", SWAP)
    out = pl.pallas_call(
        head_kernel,
        name="head",
        out_shape=jax.ShapeDtypeStruct((8, STEPS), F32),
        in_specs=[SM, ANY, ANY, VM, ANY, ANY, VM, VM, VM],
        out_specs=VM,
        scratch_shapes=[
            pltpu.VMEM((2, STEPS, HALF), BF16),
            pltpu.VMEM((2, 32, 2, 16, D), BF16),
            pltpu.VMEM((2, STEPS, HALF), BF16),
            pltpu.SemaphoreType.DMA((10,)),
        ],
        compiler_params=params(),
        cost_estimate=pl.CostEstimate(
            flops=2 * 256 * 2048 * 2432, bytes_accessed=12 << 20, transcendentals=1 << 17
        ),
    )(meta, own, pair, mixed, wd_own, wd_oth, heads, heads_oth, sel(moves)[:, None])
    here = out[:2]
    there = lax.ppermute(here, "w", SWAP)
    first = jnp.where(w == 0, here, there)
    second = jnp.where(w == 0, there, here)
    return (jnp.stack([first[0], second[0]]), jnp.stack([first[1], second[1]]))


def solution(mesh):
    fine = Mesh(mesh.devices.reshape(2, 8, 4, 2, 2), ("yh", "z", "x", "c", "w"))
    tm, batch = ("yh", "z"), ("x", "c")
    in_specs = (
        P(batch, tm),
        P(batch),
        P(batch),
        P(batch, tm, "w"),
        P(None, tm + batch, "w"),
        P(None, "w"),
        P(None, "w"),
        P("w"),
        P(tm + batch, "w"),
        P("w", None),
        P("w"),
    )
    out_specs = (P(batch, tm), P(batch, tm))
    return jax.shard_map(
        shards, mesh=fine, in_specs=in_specs, out_specs=out_specs, check_vma=False
    )
```

```python
import jax
import jax.numpy as jnp
from jax import lax
from jax.experimental import pallas as pl
from jax.experimental.pallas import tpu as pltpu
from jax.sharding import Mesh
from jax.sharding import PartitionSpec as P

D = 2048
HALF = 1024
KERNEL = 4
MOVES = 362
COLS = 384
STEPS = 256
HALO = 16
ROWS = HALO + STEPS
CH = 256
LANES = CH // 128
SEQS = 8
VMEM_LIMIT = 56 * 1024 * 1024

F32 = jnp.float32
BF16 = jnp.bfloat16
ANY = pl.BlockSpec(memory_space=pl.ANY)
VM = pl.BlockSpec(memory_space=pltpu.VMEM)
SM = pl.BlockSpec(memory_space=pltpu.SMEM)

PAIR = [(0, 1), (1, 0), (2, 3), (3, 2)]
OTHER = [(0, 3), (3, 0), (1, 2), (2, 1)]
SWAP = [(0, 1), (1, 0)]


def turn(n, k):
    return [(i, (i + k) % n) for i in range(n)]


def dot(a, b):
    return jnp.dot(a, b, preferred_element_type=F32)


def piece_copies(pieces, held, sems, w):
    mine = pl.ds(pl.multiple_of(w * HALF, HALF), HALF)
    theirs = pl.ds(pl.multiple_of((1 - w) * HALF, HALF), HALF)
    groups = []
    for block in range(2):
        for core, (own, pair, other, far0, far1) in enumerate(pieces):
            s = block * 4 + core * 2
            k = (block * 2 + core) * 3
            if block == 0:
                moved = ((own, pl.ds(s, 2), mine), (pair, pl.ds(s, 2), theirs))
            else:
                moved = ((far0, s, mine), (far1, s + 1, mine), (other, pl.ds(s, 2), theirs))
            groups.append(
                [
                    pltpu.make_async_copy(src, held.at[at, :, cols], sems.at[k + n])
                    for n, (src, at, cols) in enumerate(moved)
                ]
            )
    return groups


def weight_copies(pieces, branches, held, z, sems):
    copies = []
    for n, b in enumerate(branches):
        for h in range(2):
            for k, dz in enumerate((0, 7, 6, 5, 1, 2, 3, 4)):
                src = pieces[k].at[h, :, :, b] if k < 7 else pieces[7 + h].at[0, :, :, b]
                to = held.at[n, h, lax.rem(z + dz, 8)]
                copies.append(pltpu.make_async_copy(src, to, sems.at[n, h * 8 + k]))
    return copies


def weights_of(held, n):
    return held[n].reshape(D, CH)


def recur_kernel(meta, *refs):
    pieces = (refs[0:5], refs[5:10])
    conv_w, bias, rates = refs[19:22]
    decays, states, ends = refs[22:25]
    feat, held, ext, x_sems, w_sems = refs[25:]
    w, z, q = meta[0], meta[3], meta[4]
    to_held = weight_copies(refs[10:19], (1, 2, 3), held, z, w_sems)
    groups = piece_copies(pieces, feat, x_sems, w)
    for copy in to_held:
        copy.start()
    for group in groups:
        for copy in group:
            copy.start()
    for copy in to_held:
        copy.wait()
    chans = pl.ds(pl.multiple_of(q * CH, CH), CH)
    taps, biases, rate = conv_w[:, chans], bias[:, chans], rates[:, chans]

    def one(i, carry):
        ext[...] = dot(feat[i], weights_of(held, 0))
        conv = taps[0:1] * ext[HALO:]
        for k in range(1, KERNEL):
            conv = conv + taps[k : k + 1] * ext[HALO - k : HALO - k + STEPS]
        main = feat[i, HALO:]
        recur = jax.nn.sigmoid(dot(main, weights_of(held, 1)) + biases[0:1])
        inflow = jax.nn.sigmoid(dot(main, weights_of(held, 2)) + biases[1:2])
        decay = jnp.exp(-8.0 * recur * rate)
        drive = jnp.sqrt(1.0 - decay * decay) * inflow * conv
        for lane in range(LANES):
            cols = slice(lane * 128, (lane + 1) * 128)
            decays[lane, pl.ds(i, STEPS, stride=SEQS), :] = decay[:, cols]
            states[lane, pl.ds(i, STEPS, stride=SEQS), :] = drive[:, cols]
        return carry

    for n, group in enumerate(groups):
        for copy in group:
            copy.wait()
        lax.fori_loop(n * 2, n * 2 + 2, one, 0)

    def step(t, carry):
        at = pl.ds(pl.multiple_of(t * SEQS, SEQS), SEQS)
        done = []
        for lane, (state, product) in enumerate(carry):
            decay = decays[lane, at]
            state = decay * state + states[lane, at]
            product = product * decay
            states[lane, at] = state
            decays[lane, at] = product
            done.append((state, product))
        return tuple(done)

    start = (jnp.zeros((SEQS, 128), F32), jnp.ones((SEQS, 128), F32))
    last = lax.fori_loop(0, STEPS, step, (start,) * LANES, unroll=8)
    for lane, (state, product) in enumerate(last):
        ends[0, :, lane * 128 : (lane + 1) * 128] = product
        ends[1, :, lane * 128 : (lane + 1) * 128] = state


def gate_kernel(meta, *refs):
    pieces = (refs[0:5], refs[5:10])
    decays, states = refs[19:21]
    scaled, base = refs[22:24]
    feat, held, x_sems, w_sems = refs[24:]
    w, z = meta[0], meta[3]
    to_held = weight_copies(refs[10:19], (0,), held, z, w_sems)
    groups = piece_copies(pieces, feat, x_sems, w)
    for copy in to_held:
        copy.start()
    for group in groups:
        for copy in group:
            copy.start()
    for copy in to_held:
        copy.wait()

    def one(i, carry):
        gated = jax.nn.gelu(dot(feat[i, HALO:], weights_of(held, 0)))
        at = pl.ds(i, STEPS, stride=SEQS)
        for lane in range(LANES):
            cols = slice(lane * 128, (lane + 1) * 128)
            scaled[i, :, cols] = decays[lane, at, :] * gated[:, cols]
            base[i, :, cols] = states[lane, at, :] * gated[:, cols]
        return carry

    for n, group in enumerate(groups):
        for copy in group:
            copy.wait()
        lax.fori_loop(n * 2, n * 2 + 2, one, 0)


def mix_kernel(meta, scaled, base, blocks, mixed):
    c, yh, z = meta[1], meta[2], meta[3]
    row = lax.broadcasted_iota(jnp.int32, (SEQS, CH), 0)
    late = jnp.where(row < 4, yh, 1 - yh) == 1
    whole = jnp.zeros((SEQS, CH), F32)
    for k in range(8):
        whole = blocks[k, 0] * whole + blocks[k, 1]
    incoming = jnp.where(late, pltpu.roll(whole, 4, 0), 0.0)
    for k in range(8):
        incoming = jnp.where(k < z, blocks[k, 0] * incoming + blocks[k, 1], incoming)
    for i in range(SEQS):
        block, core, game = i // 4, (i // 2) % 2, i % 2
        yb = yh if block == 0 else 1 - yh
        cb = c if core == 0 else 1 - c
        mix = base[i] + scaled[i] * incoming[i : i + 1]
        mixed[(yb * 2 + cb) * 2 + game] = mix.astype(BF16)


def head_kernel(
    meta,
    lengths,
    outcomes,
    moves,
    own,
    pair,
    mixed,
    wd_own,
    wd_oth,
    wp_own,
    wp_oth,
    out,
    feat,
    down_w,
    resid,
    f_sems,
    w_sems,
):
    w, c, yh, z = meta[0], meta[1], meta[2], meta[3]
    to_feat = [
        pltpu.make_async_copy(own.at[w], feat.at[w], f_sems.at[0]),
        pltpu.make_async_copy(pair.at[w], feat.at[1 - w], f_sems.at[1]),
    ]
    to_down = []
    for n, rel in enumerate((((0, w), (1, 1 - w)), ((3, w), (2, 1 - w)))):
        h = yh if n == 0 else 1 - yh
        copies = []
        for src, core in ((wd_own, c), (wd_oth, 1 - c)):
            for r, v in rel:
                to = down_w.at[h, :, core, :, pl.ds(pl.multiple_of(v * HALF, HALF), HALF)]
                copies.append(
                    pltpu.make_async_copy(src.at[:, r], to, w_sems.at[n, len(copies)])
                )
        to_down.append(copies)
    for copy in to_feat + to_down[0] + to_down[1]:
        copy.start()
    order = [(h * 2 + k) * 2 + v for v in range(2) for h in range(2) for k in range(2)]
    mix = jnp.concatenate([mixed[j] for j in order], axis=1)
    for copy in to_feat:
        copy.wait()
    square = jnp.zeros((STEPS, 1), F32)
    width = 512
    for n, copies in enumerate(to_down):
        for copy in copies:
            copy.wait()
        h = yh if n == 0 else 1 - yh
        for j in range(2):
            rows = down_w[h, j * 16 : (j + 1) * 16].reshape(width, D)
            down = lax.dot_general(
                mix, rows, (((1,), (1,)), ((), ())), preferred_element_type=F32
            )
            at = slice(j * width, (j + 1) * width)
            value = (feat[h, HALO:, at].astype(F32) + down).astype(BF16)
            resid[h, :, at] = value
            wide = value.astype(F32)
            square = square + jnp.sum(wide * wide, axis=1, keepdims=True)
    raw = dot(resid[w], wp_own[...]) + dot(resid[1 - w], wp_oth[...])
    norm = lax.rsqrt(square / D + 1e-06)
    logits = raw * norm
    column = lax.broadcasted_iota(jnp.int32, logits.shape, 1)
    policy = column < MOVES
    top = jnp.max(jnp.where(policy, logits, -jnp.inf), axis=1, keepdims=True)
    total = jnp.sum(jnp.where(policy, jnp.exp(logits - top), 0.0), axis=1, keepdims=True)
    lse = top + jnp.log(total)
    played = jnp.broadcast_to(moves[pl.ds(w, 1), :].astype(F32), (128, STEPS)).T
    played = jnp.concatenate([played] * (COLS // 128), axis=1).astype(jnp.int32)
    picked = jnp.sum(jnp.where(column == played, logits, 0.0), axis=1, keepdims=True)
    score = jnp.sum(jnp.where(column == MOVES, logits, 0.0), axis=1, keepdims=True)
    value = jnp.tanh(score)
    place = (yh * 8 + z) * STEPS + lax.broadcasted_iota(jnp.int32, (STEPS, 1), 0)
    miss = value - outcomes[w].astype(F32)
    loss = jnp.where(place < lengths[w], lse - picked + miss * miss, 0.0)
    lane = lax.broadcasted_iota(jnp.int32, (STEPS, 128), 1)
    both = jnp.where(lane == 0, loss, jnp.where(lane == 1, value, 0.0))
    out[...] = both.T[0:8]


def params():
    return pltpu.CompilerParams(vmem_limit_bytes=VMEM_LIMIT)


def sent_to_all(x, axis):
    length = lax.axis_size(axis)
    return lax.all_to_all(jnp.broadcast_to(x[None], (length, *x.shape)), axis, 0, 0, tiled=True)


def shards(
    moves,
    lengths,
    outcomes,
    embedded,
    w_branches,
    conv_w,
    gate_bias,
    rates,
    w_down,
    w_policy,
    w_value,
):
    yh, z, c, w = (lax.axis_index(a) for a in ("yh", "z", "c", "w"))
    meta = jnp.stack([w, c, yh, z, yh * 2 + c]).astype(jnp.int32)
    ring = ("yh", "w")
    together = lax.optimization_barrier

    halo = lax.ppermute(embedded[:, STEPS - HALO :], ("yh", "z"), [(k, k + 1) for k in range(15)])
    quarters = w_branches.reshape(4, 16, 2, 2, CH).transpose(2, 3, 0, 1, 4)
    quarters = jnp.broadcast_to(quarters[:, None], (2, 4, 2, 4, 16, CH)).reshape(16, 4, 16, CH)
    rows = lax.all_to_all(quarters, ("yh", "x", "c"), 0, 0, tiled=True)
    halo, rows, part = together((halo, rows, w_down))
    rows = rows.reshape(2, 4, 2, 4, 16, CH)

    own = jnp.concatenate([halo, embedded], axis=1)
    parts = [part] + [lax.ppermute(part, ring, p) for p in (PAIR, OTHER, turn(4, 2))]

    def on_z(up, down):
        return lax.ppermute(up, "z", turn(8, 1)), lax.ppermute(down, "z", turn(8, 7))

    swap = lambda a: lax.ppermute(a, "c", SWAP)
    pair, other = lax.ppermute(own, ring, PAIR), lax.ppermute(own, ring, OTHER)
    up1, down1 = on_z(rows, rows)
    up2, down2 = on_z(up1, down1)
    pair, other, up2, down2, parts, here = together((pair, other, up2, down2, parts, own))
    wd_own = lax.all_gather(jnp.stack(parts), ("z", "x"), axis=0)
    far0 = lax.ppermute(other[0], ring, PAIR)
    far1 = lax.ppermute(pair[1], ring, OTHER)
    own_c = swap(here)
    up3, down3 = on_z(up2, down2)
    far0, far1, own_c, up3, down3, near, late = together((far0, far1, own_c, up3, down3, pair, other))
    low, high = on_z(up3[:1], down3[1:])
    pair_c, other_c = swap(near), swap(late)
    low, high, pair_c, other_c, gone0, gone1 = together((low, high, pair_c, other_c, far0, far1))
    far0_c, far1_c = swap(gone0), swap(gone1)
    mine = (own, pair, other, far0, far1)
    theirs = (own_c, pair_c, other_c, far0_c, far1_c)
    weights = (rows, up1, up2, up3, down1, down2, down3, low, high)

    x_scratch = pltpu.VMEM((SEQS, ROWS, D), BF16)
    decays, states, ends = pl.pallas_call(
        recur_kernel,
        name="recur",
        out_shape=(
            jax.ShapeDtypeStruct((LANES, STEPS * SEQS, 128), F32),
            jax.ShapeDtypeStruct((LANES, STEPS * SEQS, 128), F32),
            jax.ShapeDtypeStruct((2, SEQS, CH), F32),
        ),
        in_specs=[SM] + [ANY] * 19 + [VM] * 3,
        out_specs=(VM, VM, VM),
        scratch_shapes=[
            x_scratch,
            pltpu.VMEM((3, 2, 8, 4, 2, 16, CH), BF16),
            pltpu.VMEM((ROWS, CH), F32),
            pltpu.SemaphoreType.DMA((12,)),
            pltpu.SemaphoreType.DMA((3, 16)),
        ],
        compiler_params=params(),
        cost_estimate=pl.CostEstimate(
            flops=2 * 2048 * 2048 * 768, bytes_accessed=15 << 20, transcendentals=5 << 19
        ),
    )(meta, *mine, *theirs, *weights, conv_w, gate_bias, rates[None])

    heads = jnp.concatenate(
        [w_policy, w_value[:, None], jnp.zeros((HALF, COLS - MOVES - 1), BF16)], axis=1
    )
    heads, _ = lax.optimization_barrier((heads, far0))
    heads_oth = lax.ppermute(heads, "w", SWAP)
    blocks = sent_to_all(ends, "z")
    scaled, base = pl.pallas_call(
        gate_kernel,
        name="gate",
        out_shape=(
            jax.ShapeDtypeStruct((SEQS, STEPS, CH), F32),
            jax.ShapeDtypeStruct((SEQS, STEPS, CH), F32),
        ),
        in_specs=[SM] + [ANY] * 19 + [VM, VM, ANY],
        out_specs=(VM, VM),
        scratch_shapes=[
            x_scratch,
            pltpu.VMEM((1, 2, 8, 4, 2, 16, CH), BF16),
            pltpu.SemaphoreType.DMA((12,)),
            pltpu.SemaphoreType.DMA((1, 16)),
        ],
        compiler_params=params(),
        cost_estimate=pl.CostEstimate(
            flops=2 * 2048 * 2048 * 2048, bytes_accessed=60 << 20, transcendentals=1 << 19
        ),
    )(meta, *mine, *theirs, *weights, decays, states, heads_oth)

    mixed = pl.pallas_call(
        mix_kernel,
        name="mix",
        out_shape=jax.ShapeDtypeStruct((SEQS, STEPS, CH), BF16),
        in_specs=[SM] + [VM] * 3,
        out_specs=VM,
        compiler_params=params(),
        cost_estimate=pl.CostEstimate(flops=4 << 19, bytes_accessed=5 << 20, transcendentals=0),
    )(meta, scaled, base, blocks)
    wd_own, mixed = together((wd_own, mixed))
    mixed = lax.all_to_all(mixed, ("yh", "c", "w"), 0, 0, tiled=True)

    wd_oth = lax.ppermute(wd_own, "c", SWAP)
    out = pl.pallas_call(
        head_kernel,
        name="head",
        out_shape=jax.ShapeDtypeStruct((8, STEPS), F32),
        in_specs=[SM, SM, SM, VM, ANY, ANY, VM, ANY, ANY, VM, VM],
        out_specs=VM,
        scratch_shapes=[
            pltpu.VMEM((2, ROWS, HALF), BF16),
            pltpu.VMEM((2, 32, 2, 16, D), BF16),
            pltpu.VMEM((2, STEPS, HALF), BF16),
            pltpu.SemaphoreType.DMA((2,)),
            pltpu.SemaphoreType.DMA((2, 4)),
        ],
        compiler_params=params(),
        cost_estimate=pl.CostEstimate(
            flops=2 * 256 * 2048 * 2432, bytes_accessed=12 << 20, transcendentals=1 << 17
        ),
    )(meta, lengths, outcomes, moves, own, pair, mixed, wd_own, wd_oth, heads, heads_oth)
    here = out[:2]
    there = lax.ppermute(here, "w", SWAP)
    first = jnp.where(w == 0, here, there)
    second = jnp.where(w == 0, there, here)
    return (jnp.stack([first[0], second[0]]), jnp.stack([first[1], second[1]]))


def solution(mesh):
    fine = Mesh(mesh.devices.reshape(2, 8, 4, 2, 2), ("yh", "z", "x", "c", "w"))
    tm, batch = ("yh", "z"), ("x", "c")
    in_specs = (
        P(batch, tm),
        P(batch),
        P(batch),
        P(batch, tm, "w"),
        P(None, tm + batch, "w"),
        P(None, "w"),
        P(None, "w"),
        P("w"),
        P(tm + batch, "w"),
        P("w", None),
        P("w"),
    )
    out_specs = (P(batch, tm), P(batch, tm))
    return jax.shard_map(
        shards, mesh=fine, in_specs=in_specs, out_specs=out_specs, check_vma=False
    )
```

```python
import jax
import jax.numpy as jnp
from jax import lax
from jax.experimental import pallas as pl
from jax.experimental.pallas import tpu as pltpu
from jax.sharding import Mesh
from jax.sharding import PartitionSpec as P

D = 2048
HALF = 1024
KERNEL = 4
MOVES = 362
COLS = 384
STEPS = 256
HALO = 16
ROWS = HALO + STEPS
CH = 256
LANES = CH // 128
SEQS = 8
VMEM_LIMIT = 56 * 1024 * 1024

F32 = jnp.float32
BF16 = jnp.bfloat16
ANY = pl.BlockSpec(memory_space=pl.ANY)
VM = pl.BlockSpec(memory_space=pltpu.VMEM)
SM = pl.BlockSpec(memory_space=pltpu.SMEM)

PAIR = [(0, 1), (1, 0), (2, 3), (3, 2)]
OTHER = [(0, 3), (3, 0), (1, 2), (2, 1)]
SWAP = [(0, 1), (1, 0)]


def turn(n, k):
    return [(i, (i + k) % n) for i in range(n)]


def dot(a, b):
    return jnp.dot(a, b, preferred_element_type=F32)


def piece_copies(pieces, held, sems, w):
    mine = pl.ds(pl.multiple_of(w * HALF, HALF), HALF)
    theirs = pl.ds(pl.multiple_of((1 - w) * HALF, HALF), HALF)
    groups = []
    for block in range(2):
        for core, (own, pair, other, far0, far1) in enumerate(pieces):
            s = block * 4 + core * 2
            k = (block * 2 + core) * 3
            if block == 0:
                moved = ((own, pl.ds(s, 2), mine), (pair, pl.ds(s, 2), theirs))
            else:
                moved = ((far0, s, mine), (far1, s + 1, mine), (other, pl.ds(s, 2), theirs))
            groups.append(
                [
                    pltpu.make_async_copy(src, held.at[at, :, cols], sems.at[k + n])
                    for n, (src, at, cols) in enumerate(moved)
                ]
            )
    return groups


def weight_copies(pieces, first, held, x, sems):
    some = pl.ds(first, held.shape[4])
    copies = []
    for k, dx in enumerate((0, 3, 1)):
        to = held.at[:, :, lax.rem(x + dx, 4)]
        copies.append(pltpu.make_async_copy(pieces[k].at[:, :, :, some], to, sems.at[k]))
    for h in range(2):
        to = held.at[h, :, lax.rem(x + 2, 4)]
        src = pieces[3 + h].at[0, :, :, some]
        copies.append(pltpu.make_async_copy(src, to, sems.at[3 + h]))
    return copies


def weights_of(held, n):
    return held[:, :, :, :, n].reshape(D, CH)


def start(copies):
    for copy in copies:
        copy.start()


def wait(copies):
    for copy in copies:
        copy.wait()


def recur_kernel(meta, *refs):
    pieces = (refs[0:5], refs[5:10])
    conv_w, bias, rates = refs[15:18]
    decays_out, states_out, ends = refs[18:21]
    feat, held, exts, decays, states, x_sems, w_sems, out_sems = refs[21:]
    w, x, q = meta[0], meta[4], meta[2] * 2 + meta[1]
    to_held = weight_copies(refs[10:15], 1, held, x, w_sems)
    groups = piece_copies(pieces, feat, x_sems, w)
    start(groups[0] + to_held)
    start(groups[1] + groups[2] + groups[3])
    chans = pl.ds(pl.multiple_of(q * CH, CH), CH)
    taps, biases, rate = conv_w[:, chans], bias[:, chans], rates[:, chans]

    def one(i):
        ext = exts.at[i % 2]
        ext[...] = dot(feat[i], weights_of(held, 0))
        conv = taps[0:1] * ext[HALO:]
        for k in range(1, KERNEL):
            conv = conv + taps[k : k + 1] * ext[HALO - k : HALO - k + STEPS]
        main = feat[i, HALO:]
        recur = jax.nn.sigmoid(dot(main, weights_of(held, 1)) + biases[0:1])
        inflow = jax.nn.sigmoid(dot(main, weights_of(held, 2)) + biases[1:2])
        decay = jnp.exp(-8.0 * recur * rate)
        drive = jnp.sqrt(1.0 - decay * decay) * inflow * conv
        for lane in range(LANES):
            cols = slice(lane * 128, (lane + 1) * 128)
            decays[lane, pl.ds(i, STEPS, stride=SEQS), :] = decay[:, cols]
            states[lane, pl.ds(i, STEPS, stride=SEQS), :] = drive[:, cols]

    wait(to_held)
    for n, group in enumerate(groups):
        wait(group)
        one(n * 2)
        one(n * 2 + 1)

    def step(t, carry):
        at = pl.ds(pl.multiple_of(t * SEQS, SEQS), SEQS)
        done = []
        for lane, (state, product) in enumerate(carry):
            decay = decays[lane, at]
            state = decay * state + states[lane, at]
            product = product * decay
            states[lane, at] = state
            decays[lane, at] = product
            done.append((state, product))
        return tuple(done)

    last = ((jnp.zeros((SEQS, 128), F32), jnp.ones((SEQS, 128), F32)),) * LANES
    to_out = []
    for k in range(4):
        last = lax.fori_loop(k * STEPS // 4, (k + 1) * STEPS // 4, step, last, unroll=8)
        at = pl.ds(k * STEPS * SEQS // 4, STEPS * SEQS // 4)
        moved = [
            pltpu.make_async_copy(src.at[:, at], to.at[:, at], out_sems.at[k * 2 + n])
            for n, (src, to) in enumerate(((decays, decays_out), (states, states_out)))
        ]
        start(moved)
        to_out += moved
    for lane, (state, product) in enumerate(last):
        for k in range(8):
            ends[k, 0, :, lane * 128 : (lane + 1) * 128] = product
            ends[k, 1, :, lane * 128 : (lane + 1) * 128] = state
    wait(to_out)


def gate_kernel(meta, *refs):
    pieces = (refs[0:5], refs[5:10])
    decays_in, states_in = refs[15:17]
    out = refs[18]
    feat, held, decays, states, both, x_sems, w_sems, in_sems, out_sems = refs[19:]
    w, x = meta[0], meta[4]
    to_held = weight_copies(refs[10:15], 0, held, x, w_sems)
    groups = piece_copies(pieces, feat, x_sems, w)
    to_in = [
        pltpu.make_async_copy(decays_in, decays, in_sems.at[0]),
        pltpu.make_async_copy(states_in, states, in_sems.at[1]),
    ]
    start(groups[0] + to_held + to_in)
    start(groups[1] + groups[2] + groups[3])

    def moved(i):
        return pltpu.make_async_copy(both.at[i], out.at[i], out_sems.at[i])

    def one(i, carry):
        gated = jax.nn.gelu(dot(feat[i, HALO:], weights_of(held, 0)))
        at = pl.ds(i, STEPS, stride=SEQS)
        for lane in range(LANES):
            cols = slice(lane * 128, (lane + 1) * 128)
            both[i, 0, :, cols] = decays[lane, at, :] * gated[:, cols]
            both[i, 1, :, cols] = states[lane, at, :] * gated[:, cols]
        moved(i).start()
        return carry

    wait(to_held)
    for n, group in enumerate(groups):
        wait(group)
        if n == 0:
            wait(to_in)
        lax.fori_loop(n * 2, n * 2 + 2, one, 0)
    wait([moved(i) for i in range(SEQS)])


def mix_kernel(meta, gated, blocks, out, both, mixed, in_sems, out_sems):
    c, yh, z = meta[1], meta[2], meta[3]
    to_both = [
        pltpu.make_async_copy(gated.at[i], both.at[i], in_sems.at[i]) for i in range(SEQS)
    ]
    start(to_both)
    row = lax.broadcasted_iota(jnp.int32, (SEQS, CH), 0)
    late = jnp.where(row < 4, yh, 1 - yh) == 1
    whole = jnp.zeros((SEQS, CH), F32)
    for k in range(8):
        whole = blocks[k, 0] * whole + blocks[k, 1]
    incoming = jnp.where(late, pltpu.roll(whole, 4, 0), 0.0)
    for k in range(8):
        incoming = jnp.where(k < z, blocks[k, 0] * incoming + blocks[k, 1], incoming)
    to_out = []
    for i in range(SEQS):
        block, core, game = i // 4, (i // 2) % 2, i % 2
        yb = yh if block == 0 else 1 - yh
        cb = c if core == 0 else 1 - c
        to_both[i].wait()
        mixed[i] = (both[i, 1] + both[i, 0] * incoming[i : i + 1]).astype(BF16)
        to = out.at[(yb * 2 + cb) * 2 + game]
        to_out.append(pltpu.make_async_copy(mixed.at[i], to, out_sems.at[i]))
        to_out[i].start()
    wait(to_out)


def down_copies(pieces, down_w, w, c, yh, x, sems):
    column, beside, beside_c, across, across_c = pieces
    gathered = (
        (column, 0, 0),
        (beside, 3 - 2 * c, 0),
        (beside_c, 1 + 2 * c, 0),
        (across, 2, 4 * c),
        (across_c, 2, 4 - 4 * c),
    )
    groups = []
    for n, (h, rel) in enumerate(((yh, ((0, w), (1, 1 - w))), (1 - yh, ((3, w), (2, 1 - w))))):
        copies = []
        for r, v in rel:
            at = pl.ds(pl.multiple_of(v * HALF, HALF), HALF)
            for src, dx, first in gathered:
                to = down_w.at[h, pl.ds(first, src.shape[0]), lax.rem(x + dx, 4), :, :, at]
                sem = sems.at[n, len(copies)]
                copies.append(pltpu.make_async_copy(src.at[:, :, r], to, sem))
        groups.append(copies)
    return groups


def head_kernel(
    meta,
    lengths,
    outcomes,
    moves,
    own,
    pair,
    mixed,
    column,
    beside,
    beside_c,
    across,
    across_c,
    heads,
    heads_oth,
    out,
    feat,
    mix,
    down_w,
    resid,
    wp,
    f_sems,
    m_sems,
    d_sems,
):
    w, c, yh, z, x = meta[0], meta[1], meta[2], meta[3], meta[4]
    to_mix = []
    for j in range(SEQS):
        to = mix.at[:, pl.ds((j % 2) * HALF + (j // 2) * CH, CH)]
        to_mix.append(pltpu.make_async_copy(mixed.at[j], to, m_sems.at[j]))
    pieces = (column, beside, beside_c, across, across_c)
    to_down = down_copies(pieces, down_w, w, c, yh, x, d_sems)
    to_feat = [
        pltpu.make_async_copy(own.at[w], feat.at[w], f_sems.at[0]),
        pltpu.make_async_copy(pair.at[w], feat.at[1 - w], f_sems.at[1]),
    ]
    to_wp = [
        pltpu.make_async_copy(heads, wp.at[w], f_sems.at[2]),
        pltpu.make_async_copy(heads_oth, wp.at[1 - w], f_sems.at[3]),
    ]
    start(to_mix + to_down[0] + to_feat + to_down[1] + to_wp)
    wait(to_mix)
    square = jnp.zeros((STEPS, 1), F32)
    width = 512
    for k in range(4):
        h, j = (yh if k < 2 else 1 - yh), k % 2
        if j == 0:
            wait(to_down[k // 2])
        rows = down_w[h, j * 4 : (j + 1) * 4].reshape(width, D)
        down = lax.dot_general(
            mix[...], rows, (((1,), (1,)), ((), ())), preferred_element_type=F32
        )
        if k == 0:
            wait(to_feat)
        at = slice(j * width, (j + 1) * width)
        value = (feat[h, HALO:, at].astype(F32) + down).astype(BF16)
        resid[h, :, at] = value
        wide = value.astype(F32)
        square = square + jnp.sum(wide * wide, axis=1, keepdims=True)
    wait(to_wp)
    raw = dot(resid[0], wp[0]) + dot(resid[1], wp[1])
    norm = lax.rsqrt(square / D + 1e-06)
    logits = raw * norm
    column = lax.broadcasted_iota(jnp.int32, logits.shape, 1)
    policy = column < MOVES
    top = jnp.max(jnp.where(policy, logits, -jnp.inf), axis=1, keepdims=True)
    total = jnp.sum(jnp.where(policy, jnp.exp(logits - top), 0.0), axis=1, keepdims=True)
    lse = top + jnp.log(total)
    played = jnp.broadcast_to(moves[pl.ds(w, 1), :].astype(F32), (128, STEPS)).T
    played = jnp.concatenate([played] * (COLS // 128), axis=1).astype(jnp.int32)
    picked = jnp.sum(jnp.where(column == played, logits, 0.0), axis=1, keepdims=True)
    score = jnp.sum(jnp.where(column == MOVES, logits, 0.0), axis=1, keepdims=True)
    value = jnp.tanh(score)
    place = (yh * 8 + z) * STEPS + lax.broadcasted_iota(jnp.int32, (STEPS, 1), 0)
    miss = value - outcomes[w].astype(F32)
    loss = jnp.where(place < lengths[w], lse - picked + miss * miss, 0.0)
    lane = lax.broadcasted_iota(jnp.int32, (STEPS, 128), 1)
    both = jnp.where(lane == 0, loss, jnp.where(lane == 1, value, 0.0))
    out[...] = both.T[0:2]


def params():
    return pltpu.CompilerParams(vmem_limit_bytes=VMEM_LIMIT)


def shards(
    moves,
    lengths,
    outcomes,
    embedded,
    w_branches,
    conv_w,
    gate_bias,
    rates,
    w_down,
    w_policy,
    w_value,
):
    yh, z, x, c, w = (lax.axis_index(a) for a in ("yh", "z", "x", "c", "w"))
    meta = jnp.stack([w, c, yh, z, x]).astype(jnp.int32)
    ring = ("yh", "w")
    together = lax.optimization_barrier

    halo = lax.ppermute(embedded[:, STEPS - HALO :], ("yh", "z"), [(k, k + 1) for k in range(15)])
    quarters = w_branches.reshape(4, 16, 2, 2, CH).transpose(2, 3, 0, 1, 4)
    quarters = jnp.broadcast_to(quarters[:, None], (2, 8, 2, 4, 16, CH)).reshape(32, 4, 16, CH)
    rows = lax.all_to_all(quarters, ("yh", "z", "c"), 0, 0, tiled=True)
    rows = rows.reshape(2, 8, 2, 4, 16, CH)
    parts = [w_down] + [lax.ppermute(w_down, ring, p) for p in (PAIR, OTHER, turn(4, 2))]
    halo, parts = together((halo, parts))

    own = jnp.concatenate([halo, embedded], axis=1)
    column = lax.all_gather(jnp.stack(parts), ("z", "c"), axis=0).reshape(8, 2, 4, 16, HALF)
    swap = lambda a: lax.ppermute(a, "c", SWAP)
    pair, other = lax.ppermute(own, ring, PAIR), lax.ppermute(own, ring, OTHER)
    behind, ahead = lax.ppermute(rows, "x", turn(4, 1)), lax.ppermute(rows, "x", turn(4, 3))
    own_c = swap(own)
    heads = jnp.concatenate(
        [w_policy, w_value[:, None], jnp.zeros((HALF, COLS - MOVES - 1), BF16)], axis=1
    )
    pair, other, behind, ahead, own_c, heads, pair_half, other_half, meta = together(
        (pair, other, behind, ahead, own_c, heads, pair[1], other[0], meta)
    )
    far0 = lax.ppermute(other_half, ring, PAIR)
    far1 = lax.ppermute(pair_half, ring, OTHER)
    low = lax.ppermute(behind[:1], "x", turn(4, 1))
    high = lax.ppermute(ahead[1:], "x", turn(4, 3))
    pair_c = swap(pair)
    far0, far1, low, high, pair_c, late, column = together(
        (far0, far1, low, high, pair_c, other, column)
    )
    apart = [(k, (k + 2 if k % 2 == 0 else k - 2) % 8) for k in range(8)]
    other_c, far0_c, far1_c = swap(late), swap(far0), swap(far1)
    beside = lax.ppermute(column, ("x", "c"), apart)
    mine = (own, pair, other, far0, far1)
    theirs = (own_c, pair_c, other_c, far0_c, far1_c)
    weights = (rows, behind, ahead, low, high)

    x_scratch = pltpu.VMEM((SEQS, ROWS, D), BF16)
    w_scratch = lambda n: pltpu.VMEM((2, 8, 4, 2, n, 16, CH), BF16)
    by_step = (LANES, STEPS * SEQS, 128)
    sems = lambda n: pltpu.SemaphoreType.DMA((n,))
    decays, states, ends = pl.pallas_call(
        recur_kernel,
        name="recur",
        out_shape=(
            jax.ShapeDtypeStruct(by_step, F32),
            jax.ShapeDtypeStruct(by_step, F32),
            jax.ShapeDtypeStruct((8, 2, SEQS, CH), F32),
        ),
        in_specs=[SM] + [ANY] * 15 + [VM] * 3,
        out_specs=(ANY, ANY, VM),
        scratch_shapes=[
            x_scratch,
            w_scratch(3),
            pltpu.VMEM((2, ROWS, CH), F32),
            pltpu.VMEM(by_step, F32),
            pltpu.VMEM(by_step, F32),
            sems(12),
            sems(5),
            sems(8),
        ],
        compiler_params=params(),
        cost_estimate=pl.CostEstimate(
            flops=2 * 2048 * 2048 * 768, bytes_accessed=15 << 20, transcendentals=5 << 19
        ),
    )(meta, *mine, *theirs, *weights, conv_w, gate_bias, rates[None])

    beside, _ = together((beside, ends))
    beside_c = swap(beside)
    across = lax.dynamic_slice_in_dim(beside, c * 4, 4, 0)
    across = lax.ppermute(across, ("x", "c"), apart)
    heads, _ = together((heads, far0))
    heads_oth = lax.ppermute(heads, "w", SWAP)
    blocks = lax.all_to_all(ends, "z", 0, 0, tiled=True)
    gated = pl.pallas_call(
        gate_kernel,
        name="gate",
        out_shape=jax.ShapeDtypeStruct((SEQS, 2, STEPS, CH), F32),
        in_specs=[SM] + [ANY] * 18,
        out_specs=ANY,
        scratch_shapes=[
            x_scratch,
            w_scratch(1),
            pltpu.VMEM(by_step, F32),
            pltpu.VMEM(by_step, F32),
            pltpu.VMEM((SEQS, 2, STEPS, CH), F32),
            sems(12),
            sems(5),
            sems(2),
            sems(8),
        ],
        compiler_params=params(),
        cost_estimate=pl.CostEstimate(
            flops=2 * 2048 * 2048 * 2048, bytes_accessed=60 << 20, transcendentals=1 << 19
        ),
    )(meta, *mine, *theirs, *weights, decays, states, heads_oth)

    mixed = pl.pallas_call(
        mix_kernel,
        name="mix",
        out_shape=jax.ShapeDtypeStruct((SEQS, STEPS, CH), BF16),
        in_specs=[SM, ANY, VM],
        out_specs=ANY,
        scratch_shapes=[
            pltpu.VMEM((SEQS, 2, STEPS, CH), F32),
            pltpu.VMEM((SEQS, STEPS, CH), BF16),
            sems(8),
            sems(8),
        ],
        compiler_params=params(),
        cost_estimate=pl.CostEstimate(flops=4 << 19, bytes_accessed=5 << 20, transcendentals=0),
    )(meta, gated, blocks)
    across, mixed = together((across, mixed))
    across_c = swap(across)
    mixed = lax.all_to_all(mixed, ("yh", "c", "w"), 0, 0, tiled=True)

    out = pl.pallas_call(
        head_kernel,
        name="head",
        out_shape=jax.ShapeDtypeStruct((2, STEPS), F32),
        in_specs=[SM, SM, SM, VM] + [ANY] * 10,
        out_specs=VM,
        scratch_shapes=[
            pltpu.VMEM((2, ROWS, HALF), BF16),
            pltpu.VMEM((STEPS, D), BF16),
            pltpu.VMEM((2, 8, 4, 2, 16, D), BF16),
            pltpu.VMEM((2, STEPS, HALF), BF16),
            pltpu.VMEM((2, HALF, COLS), BF16),
            sems(4),
            sems(8),
            pltpu.SemaphoreType.DMA((2, 10)),
        ],
        compiler_params=params(),
        cost_estimate=pl.CostEstimate(
            flops=2 * 256 * 2048 * 2432, bytes_accessed=12 << 20, transcendentals=1 << 17
        ),
    )(meta, lengths, outcomes, moves, own, pair, mixed, column, beside, beside_c, across, across_c, heads, heads_oth)
    here = out
    there = lax.ppermute(here, "w", SWAP)
    game = lax.broadcasted_iota(jnp.int32, (2, STEPS), 0) == w
    return (jnp.where(game, here[:1], there[:1]), jnp.where(game, here[1:], there[1:]))


def solution(mesh):
    fine = Mesh(mesh.devices.reshape(2, 8, 4, 2, 2), ("yh", "z", "x", "c", "w"))
    tm, batch = ("yh", "z"), ("x", "c")
    in_specs = (
        P(batch, tm),
        P(batch),
        P(batch),
        P(batch, tm, "w"),
        P(None, tm + batch, "w"),
        P(None, "w"),
        P(None, "w"),
        P("w"),
        P(tm + batch, "w"),
        P("w", None),
        P("w"),
    )
    out_specs = (P(batch, tm), P(batch, tm))
    return jax.shard_map(
        shards, mesh=fine, in_specs=in_specs, out_specs=out_specs, check_vma=False
    )
```

```python
import jax
import jax.numpy as jnp
from jax import lax
from jax.experimental import pallas as pl
from jax.experimental.pallas import tpu as pltpu
from jax.sharding import Mesh
from jax.sharding import PartitionSpec as P

D = 2048
HALF = 1024
KERNEL = 4
MOVES = 362
COLS = 384
STEPS = 256
HALO = 16
ROWS = HALO + STEPS
CH = 256
LANES = CH // 128
SEQS = 8
VMEM_LIMIT = 56 * 1024 * 1024

F32 = jnp.float32
BF16 = jnp.bfloat16
ANY = pl.BlockSpec(memory_space=pl.ANY)
VM = pl.BlockSpec(memory_space=pltpu.VMEM)
SM = pl.BlockSpec(memory_space=pltpu.SMEM)

PAIR = [(0, 1), (1, 0), (2, 3), (3, 2)]
OTHER = [(0, 3), (3, 0), (1, 2), (2, 1)]
SWAP = [(0, 1), (1, 0)]


def turn(n, k):
    return [(i, (i + k) % n) for i in range(n)]


def dot(a, b):
    return jnp.dot(a, b, preferred_element_type=F32)


def piece_copies(pieces, held, sems, w, skip=0):
    mine = pl.ds(pl.multiple_of(w * HALF, HALF), HALF)
    theirs = pl.ds(pl.multiple_of((1 - w) * HALF, HALF), HALF)
    groups = []
    for block in range(2):
        for core, (own, pair, other, far0, far1) in enumerate(pieces):
            s = block * 4 + core * 2
            k = (block * 2 + core) * 3
            if block == 0:
                moved = ((own, pl.ds(s, 2), mine), (pair, pl.ds(s, 2), theirs))
            else:
                moved = ((far0, s, mine), (far1, s + 1, mine), (other, pl.ds(s, 2), theirs))
            groups.append(
                [
                    pltpu.make_async_copy(
                        src.at[..., pl.ds(skip, ROWS - skip), :], held.at[at, :, cols], sems.at[k + n]
                    )
                    for n, (src, at, cols) in enumerate(moved)
                ]
            )
    return groups


def weight_copies(pieces, first, held, x, sems):
    some = pl.ds(first, held.shape[4])
    copies = []
    for k, dx in enumerate((0, 3, 1)):
        to = held.at[:, :, lax.rem(x + dx, 4)]
        copies.append(pltpu.make_async_copy(pieces[k].at[:, :, :, some], to, sems.at[k]))
    for h in range(2):
        to = held.at[h, :, lax.rem(x + 2, 4)]
        src = pieces[3 + h].at[0, :, :, some]
        copies.append(pltpu.make_async_copy(src, to, sems.at[3 + h]))
    return copies


def weights_of(held, n):
    return held[:, :, :, :, n].reshape(D, CH)


def start(copies):
    for copy in copies:
        copy.start()


def wait(copies):
    for copy in copies:
        copy.wait()


def recur_kernel(meta, *refs):
    pieces = (refs[0:5], refs[5:10])
    conv_w, bias, rates = refs[15:18]
    decays_out, states_out, ends = refs[18:21]
    feat, held, exts, decays, states, x_sems, w_sems, out_sems = refs[21:]
    w, x, q = meta[0], meta[4], meta[2] * 2 + meta[1]
    to_held = weight_copies(refs[10:15], 1, held, x, w_sems)
    groups = piece_copies(pieces, feat, x_sems, w)
    start(groups[0] + to_held)
    start(groups[1] + groups[2] + groups[3])
    chans = pl.ds(pl.multiple_of(q * CH, CH), CH)
    taps, biases, rate = conv_w[:, chans], bias[:, chans], rates[:, chans]

    def one(i):
        ext = exts.at[i % 2]
        ext[...] = dot(feat[i], weights_of(held, 0))
        conv = taps[0:1] * ext[HALO:]
        for k in range(1, KERNEL):
            conv = conv + taps[k : k + 1] * ext[HALO - k : HALO - k + STEPS]
        main = feat[i, HALO:]
        recur = jax.nn.sigmoid(dot(main, weights_of(held, 1)) + biases[0:1])
        inflow = jax.nn.sigmoid(dot(main, weights_of(held, 2)) + biases[1:2])
        decay = jnp.exp(-8.0 * recur * rate)
        drive = jnp.sqrt(1.0 - decay * decay) * inflow * conv
        for lane in range(LANES):
            cols = slice(lane * 128, (lane + 1) * 128)
            decays[lane, pl.ds(i, STEPS, stride=SEQS), :] = decay[:, cols]
            states[lane, pl.ds(i, STEPS, stride=SEQS), :] = drive[:, cols]

    wait(to_held)
    for n, group in enumerate(groups):
        wait(group)
        one(n * 2)
        one(n * 2 + 1)

    def step(t, carry):
        at = pl.ds(pl.multiple_of(t * SEQS, SEQS), SEQS)
        done = []
        for lane, (state, product) in enumerate(carry):
            decay = decays[lane, at]
            state = decay * state + states[lane, at]
            product = product * decay
            states[lane, at] = state
            decays[lane, at] = product
            done.append((state, product))
        return tuple(done)

    last = ((jnp.zeros((SEQS, 128), F32), jnp.ones((SEQS, 128), F32)),) * LANES
    to_out = []
    for k in range(4):
        last = lax.fori_loop(k * STEPS // 4, (k + 1) * STEPS // 4, step, last, unroll=8)
        at = pl.ds(k * STEPS * SEQS // 4, STEPS * SEQS // 4)
        moved = [
            pltpu.make_async_copy(src.at[:, at], to.at[:, at], out_sems.at[k * 2 + n])
            for n, (src, to) in enumerate(((decays, decays_out), (states, states_out)))
        ]
        start(moved)
        to_out += moved
    for lane, (state, product) in enumerate(last):
        for k in range(8):
            ends[k, 0, :, lane * 128 : (lane + 1) * 128] = product
            ends[k, 1, :, lane * 128 : (lane + 1) * 128] = state
    wait(to_out)


def gate_kernel(meta, *refs):
    pieces = (refs[0:5], refs[5:10])
    decays_in, states_in = refs[15:17]
    out = refs[18]
    feat, held, decays, states, both, x_sems, w_sems, in_sems, out_sems = refs[19:]
    w, x = meta[0], meta[4]
    to_held = weight_copies(refs[10:15], 0, held, x, w_sems)
    groups = piece_copies(pieces, feat, x_sems, w, HALO)
    to_in = [
        pltpu.make_async_copy(decays_in, decays, in_sems.at[0]),
        pltpu.make_async_copy(states_in, states, in_sems.at[1]),
    ]
    start(groups[0] + to_held + to_in)
    start(groups[1] + groups[2] + groups[3])

    def moved(i):
        return pltpu.make_async_copy(both.at[i], out.at[i], out_sems.at[i])

    def one(i):
        gated = jax.nn.gelu(dot(feat[i], weights_of(held, 0)))
        at = pl.ds(i, STEPS, stride=SEQS)
        for lane in range(LANES):
            cols = slice(lane * 128, (lane + 1) * 128)
            both[i, 0, :, cols] = decays[lane, at, :] * gated[:, cols]
            both[i, 1, :, cols] = states[lane, at, :] * gated[:, cols]
        moved(i).start()

    wait(to_held)
    for n, group in enumerate(groups):
        wait(group)
        if n == 0:
            wait(to_in)
        one(n * 2)
        one(n * 2 + 1)
    wait([moved(i) for i in range(SEQS)])


def mix_kernel(meta, gated, blocks, out, both, mixed, in_sems, out_sems):
    c, yh, z = meta[1], meta[2], meta[3]
    to_both = [
        pltpu.make_async_copy(gated.at[i], both.at[i], in_sems.at[i]) for i in range(SEQS)
    ]
    start(to_both)
    row = lax.broadcasted_iota(jnp.int32, (SEQS, CH), 0)
    late = jnp.where(row < 4, yh, 1 - yh) == 1
    whole = jnp.zeros((SEQS, CH), F32)
    for k in range(8):
        whole = blocks[k, 0] * whole + blocks[k, 1]
    incoming = jnp.where(late, pltpu.roll(whole, 4, 0), 0.0)
    for k in range(8):
        incoming = jnp.where(k < z, blocks[k, 0] * incoming + blocks[k, 1], incoming)
    to_out = []
    for i in range(SEQS):
        block, core, game = i // 4, (i // 2) % 2, i % 2
        yb = yh if block == 0 else 1 - yh
        cb = c if core == 0 else 1 - c
        to_both[i].wait()
        mixed[i] = (both[i, 1] + both[i, 0] * incoming[i : i + 1]).astype(BF16)
        to = out.at[(yb * 2 + cb) * 2 + game]
        to_out.append(pltpu.make_async_copy(mixed.at[i], to, out_sems.at[i]))
        to_out[i].start()
    wait(to_out)


def down_copies(pieces, down_w, w, c, yh, x, sems):
    column, beside, beside_c, across, across_c = pieces
    gathered = (
        (column, 0, 0),
        (beside, 3 - 2 * c, 0),
        (beside_c, 1 + 2 * c, 0),
        (across, 2, 4 * c),
        (across_c, 2, 4 - 4 * c),
    )
    groups = []
    for n, (h, rel) in enumerate(((yh, ((0, w), (1, 1 - w))), (1 - yh, ((3, w), (2, 1 - w))))):
        copies = []
        for r, v in rel:
            at = pl.ds(pl.multiple_of(v * HALF, HALF), HALF)
            for src, dx, first in gathered:
                to = down_w.at[h, pl.ds(first, src.shape[0]), lax.rem(x + dx, 4), :, :, at]
                sem = sems.at[n, len(copies)]
                copies.append(pltpu.make_async_copy(src.at[:, :, r], to, sem))
        groups.append(copies)
    return groups


def head_kernel(
    meta,
    lengths,
    outcomes,
    moves,
    own,
    pair,
    mixed,
    column,
    beside,
    beside_c,
    across,
    across_c,
    heads,
    heads_oth,
    out,
    feat,
    mix,
    down_w,
    resid,
    wp,
    f_sems,
    m_sems,
    d_sems,
):
    w, c, yh, z, x = meta[0], meta[1], meta[2], meta[3], meta[4]
    to_mix = []
    for j in range(SEQS):
        to = mix.at[:, pl.ds((j % 2) * HALF + (j // 2) * CH, CH)]
        to_mix.append(pltpu.make_async_copy(mixed.at[j], to, m_sems.at[j]))
    pieces = (column, beside, beside_c, across, across_c)
    to_down = down_copies(pieces, down_w, w, c, yh, x, d_sems)
    to_feat = [
        pltpu.make_async_copy(own.at[w], feat.at[w], f_sems.at[0]),
        pltpu.make_async_copy(pair.at[w], feat.at[1 - w], f_sems.at[1]),
    ]
    to_wp = [
        pltpu.make_async_copy(heads, wp.at[w], f_sems.at[2]),
        pltpu.make_async_copy(heads_oth, wp.at[1 - w], f_sems.at[3]),
    ]
    start(to_mix + to_down[0] + to_feat + to_down[1] + to_wp)
    wait(to_mix)
    square = jnp.zeros((STEPS, 1), F32)
    width = 512
    for k in range(4):
        h, j = (yh if k < 2 else 1 - yh), k % 2
        if j == 0:
            wait(to_down[k // 2])
        rows = down_w[h, j * 4 : (j + 1) * 4].reshape(width, D)
        down = lax.dot_general(
            mix[...], rows, (((1,), (1,)), ((), ())), preferred_element_type=F32
        )
        if k == 0:
            wait(to_feat)
        at = slice(j * width, (j + 1) * width)
        value = (feat[h, HALO:, at].astype(F32) + down).astype(BF16)
        resid[h, :, at] = value
        wide = value.astype(F32)
        square = square + jnp.sum(wide * wide, axis=1, keepdims=True)
    wait(to_wp)
    raw = dot(resid[0], wp[0]) + dot(resid[1], wp[1])
    norm = lax.rsqrt(square / D + 1e-06)
    logits = raw * norm
    column = lax.broadcasted_iota(jnp.int32, logits.shape, 1)
    policy = column < MOVES
    top = jnp.max(jnp.where(policy, logits, -jnp.inf), axis=1, keepdims=True)
    total = jnp.sum(jnp.where(policy, jnp.exp(logits - top), 0.0), axis=1, keepdims=True)
    lse = top + jnp.log(total)
    played = jnp.broadcast_to(moves[pl.ds(w, 1), :].astype(F32), (128, STEPS)).T
    played = jnp.concatenate([played] * (COLS // 128), axis=1).astype(jnp.int32)
    picked = jnp.sum(jnp.where(column == played, logits, 0.0), axis=1, keepdims=True)
    score = jnp.sum(jnp.where(column == MOVES, logits, 0.0), axis=1, keepdims=True)
    value = jnp.tanh(score)
    place = (yh * 8 + z) * STEPS + lax.broadcasted_iota(jnp.int32, (STEPS, 1), 0)
    miss = value - outcomes[w].astype(F32)
    loss = jnp.where(place < lengths[w], lse - picked + miss * miss, 0.0)
    lane = lax.broadcasted_iota(jnp.int32, (STEPS, 128), 1)
    both = jnp.where(lane == 0, loss, jnp.where(lane == 1, value, 0.0))
    out[...] = both.T[0:2]


def params():
    return pltpu.CompilerParams(vmem_limit_bytes=VMEM_LIMIT)


def shards(
    moves,
    lengths,
    outcomes,
    embedded,
    w_branches,
    conv_w,
    gate_bias,
    rates,
    w_down,
    w_policy,
    w_value,
):
    yh, z, x, c, w = (lax.axis_index(a) for a in ("yh", "z", "x", "c", "w"))
    meta = jnp.stack([w, c, yh, z, x]).astype(jnp.int32)
    ring = ("yh", "w")
    together = lax.optimization_barrier

    halo = lax.ppermute(embedded[:, STEPS - HALO :], ("yh", "z"), [(k, k + 1) for k in range(15)])
    quarters = w_branches.reshape(4, 16, 2, 2, CH).transpose(2, 3, 0, 1, 4)
    quarters = jnp.broadcast_to(quarters[:, None], (2, 8, 2, 4, 16, CH)).reshape(32, 4, 16, CH)
    rows = lax.all_to_all(quarters, ("yh", "z", "c"), 0, 0, tiled=True)
    rows = rows.reshape(2, 8, 2, 4, 16, CH)
    parts = [w_down] + [lax.ppermute(w_down, ring, p) for p in (PAIR, OTHER, turn(4, 2))]
    halo, parts = together((halo, parts))

    own = jnp.concatenate([halo, embedded], axis=1)
    column = lax.all_gather(jnp.stack(parts), ("z", "c"), axis=0).reshape(8, 2, 4, 16, HALF)
    swap = lambda a: lax.ppermute(a, "c", SWAP)
    pair, other = lax.ppermute(own, ring, PAIR), lax.ppermute(own, ring, OTHER)
    behind, ahead = lax.ppermute(rows, "x", turn(4, 1)), lax.ppermute(rows, "x", turn(4, 3))
    own_c = swap(own)
    heads = jnp.concatenate(
        [w_policy, w_value[:, None], jnp.zeros((HALF, COLS - MOVES - 1), BF16)], axis=1
    )
    pair, other, behind, ahead, own_c, heads, pair_half, other_half, meta = together(
        (pair, other, behind, ahead, own_c, heads, pair[1], other[0], meta)
    )
    far0 = lax.ppermute(other_half, ring, PAIR)
    far1 = lax.ppermute(pair_half, ring, OTHER)
    low = lax.ppermute(behind[:1], "x", turn(4, 1))
    high = lax.ppermute(ahead[1:], "x", turn(4, 3))
    pair_c = swap(pair)
    far0, far1, low, high, pair_c, late, column = together(
        (far0, far1, low, high, pair_c, other, column)
    )
    apart = [(k, (k + 2 if k % 2 == 0 else k - 2) % 8) for k in range(8)]
    other_c, far0_c, far1_c = swap(late), swap(far0), swap(far1)
    beside = lax.ppermute(column, ("x", "c"), apart)
    mine = (own, pair, other, far0, far1)
    theirs = (own_c, pair_c, other_c, far0_c, far1_c)
    weights = (rows, behind, ahead, low, high)

    x_scratch = pltpu.VMEM((SEQS, ROWS, D), BF16)
    w_scratch = lambda n: pltpu.VMEM((2, 8, 4, 2, n, 16, CH), BF16)
    by_step = (LANES, STEPS * SEQS, 128)
    sems = lambda n: pltpu.SemaphoreType.DMA((n,))
    decays, states, ends = pl.pallas_call(
        recur_kernel,
        name="recur",
        out_shape=(
            jax.ShapeDtypeStruct(by_step, F32),
            jax.ShapeDtypeStruct(by_step, F32),
            jax.ShapeDtypeStruct((8, 2, SEQS, CH), F32),
        ),
        in_specs=[SM] + [ANY] * 15 + [VM] * 3,
        out_specs=(ANY, ANY, VM),
        scratch_shapes=[
            x_scratch,
            w_scratch(3),
            pltpu.VMEM((2, ROWS, CH), F32),
            pltpu.VMEM(by_step, F32),
            pltpu.VMEM(by_step, F32),
            sems(12),
            sems(5),
            sems(8),
        ],
        compiler_params=params(),
        cost_estimate=pl.CostEstimate(
            flops=2 * 2048 * 2048 * 768, bytes_accessed=15 << 20, transcendentals=5 << 19
        ),
    )(meta, *mine, *theirs, *weights, conv_w, gate_bias, rates[None])

    beside, _ = together((beside, ends))
    beside_c = swap(beside)
    across = lax.dynamic_slice_in_dim(beside, c * 4, 4, 0)
    across = lax.ppermute(across, ("x", "c"), apart)
    heads, _ = together((heads, far0))
    heads_oth = lax.ppermute(heads, "w", SWAP)
    blocks = lax.all_to_all(ends, "z", 0, 0, tiled=True)
    gated = pl.pallas_call(
        gate_kernel,
        name="gate",
        out_shape=jax.ShapeDtypeStruct((SEQS, 2, STEPS, CH), F32),
        in_specs=[SM] + [ANY] * 18,
        out_specs=ANY,
        scratch_shapes=[
            pltpu.VMEM((SEQS, STEPS, D), BF16),
            w_scratch(1),
            pltpu.VMEM(by_step, F32),
            pltpu.VMEM(by_step, F32),
            pltpu.VMEM((SEQS, 2, STEPS, CH), F32),
            sems(12),
            sems(5),
            sems(2),
            sems(8),
        ],
        compiler_params=params(),
        cost_estimate=pl.CostEstimate(
            flops=2 * 2048 * 2048 * 2048, bytes_accessed=60 << 20, transcendentals=1 << 19
        ),
    )(meta, *mine, *theirs, *weights, decays, states, heads_oth)

    mixed = pl.pallas_call(
        mix_kernel,
        name="mix",
        out_shape=jax.ShapeDtypeStruct((SEQS, STEPS, CH), BF16),
        in_specs=[SM, ANY, VM],
        out_specs=ANY,
        scratch_shapes=[
            pltpu.VMEM((SEQS, 2, STEPS, CH), F32),
            pltpu.VMEM((SEQS, STEPS, CH), BF16),
            sems(8),
            sems(8),
        ],
        compiler_params=params(),
        cost_estimate=pl.CostEstimate(flops=4 << 19, bytes_accessed=5 << 20, transcendentals=0),
    )(meta, gated, blocks)
    across, mixed = together((across, mixed))
    across_c = swap(across)
    mixed = lax.all_to_all(mixed, ("yh", "c", "w"), 0, 0, tiled=True)

    out = pl.pallas_call(
        head_kernel,
        name="head",
        out_shape=jax.ShapeDtypeStruct((2, STEPS), F32),
        in_specs=[SM, SM, SM, VM] + [ANY] * 10,
        out_specs=VM,
        scratch_shapes=[
            pltpu.VMEM((2, ROWS, HALF), BF16),
            pltpu.VMEM((STEPS, D), BF16),
            pltpu.VMEM((2, 8, 4, 2, 16, D), BF16),
            pltpu.VMEM((2, STEPS, HALF), BF16),
            pltpu.VMEM((2, HALF, COLS), BF16),
            sems(4),
            sems(8),
            pltpu.SemaphoreType.DMA((2, 10)),
        ],
        compiler_params=params(),
        cost_estimate=pl.CostEstimate(
            flops=2 * 256 * 2048 * 2432, bytes_accessed=12 << 20, transcendentals=1 << 17
        ),
    )(meta, lengths, outcomes, moves, own, pair, mixed, column, beside, beside_c, across, across_c, heads, heads_oth)
    here = out
    there = lax.ppermute(here, "w", SWAP)
    game = lax.broadcasted_iota(jnp.int32, (2, STEPS), 0) == w
    return (jnp.where(game, here[:1], there[:1]), jnp.where(game, here[1:], there[1:]))


def solution(mesh):
    fine = Mesh(mesh.devices.reshape(2, 8, 4, 2, 2), ("yh", "z", "x", "c", "w"))
    tm, batch = ("yh", "z"), ("x", "c")
    in_specs = (
        P(batch, tm),
        P(batch),
        P(batch),
        P(batch, tm, "w"),
        P(None, tm + batch, "w"),
        P(None, "w"),
        P(None, "w"),
        P("w"),
        P(tm + batch, "w"),
        P("w", None),
        P("w"),
    )
    out_specs = (P(batch, tm), P(batch, tm))
    return jax.shard_map(
        shards, mesh=fine, in_specs=in_specs, out_specs=out_specs, check_vma=False
    )
```

```python
import jax
import jax.numpy as jnp
from jax import lax
from jax.experimental import pallas as pl
from jax.experimental.pallas import tpu as pltpu
from jax.sharding import Mesh
from jax.sharding import PartitionSpec as P

D = 2048
HALF = 1024
KERNEL = 4
MOVES = 362
COLS = 384
STEPS = 256
HALO = 16
ROWS = HALO + STEPS
CH = 256
LANES = CH // 128
SEQS = 8
VMEM_LIMIT = 56 * 1024 * 1024

F32 = jnp.float32
BF16 = jnp.bfloat16
ANY = pl.BlockSpec(memory_space=pl.ANY)
VM = pl.BlockSpec(memory_space=pltpu.VMEM)
SM = pl.BlockSpec(memory_space=pltpu.SMEM)

PAIR = [(0, 1), (1, 0), (2, 3), (3, 2)]
OTHER = [(0, 3), (3, 0), (1, 2), (2, 1)]
SWAP = [(0, 1), (1, 0)]


def turn(n, k):
    return [(i, (i + k) % n) for i in range(n)]


def dot(a, b):
    return jnp.dot(a, b, preferred_element_type=F32)


def piece_copies(pieces, held, sems, w, skip=0):
    mine = pl.ds(pl.multiple_of(w * HALF, HALF), HALF)
    theirs = pl.ds(pl.multiple_of((1 - w) * HALF, HALF), HALF)
    groups = []
    for block in range(2):
        for core, (own, pair, other, far0, far1) in enumerate(pieces):
            s = block * 4 + core * 2
            k = (block * 2 + core) * 3
            if block == 0:
                moved = ((own, pl.ds(s, 2), mine), (pair, pl.ds(s, 2), theirs))
            else:
                moved = ((far0, s, mine), (far1, s + 1, mine), (other, pl.ds(s, 2), theirs))
            groups.append(
                [
                    pltpu.make_async_copy(
                        src.at[..., pl.ds(skip, ROWS - skip), :], held.at[at, :, cols], sems.at[k + n]
                    )
                    for n, (src, at, cols) in enumerate(moved)
                ]
            )
    return groups


def weight_copies(pieces, first, held, x, sems):
    some = pl.ds(first, held.shape[4])
    copies = []
    for k, dx in enumerate((0, 3, 1)):
        to = held.at[:, :, lax.rem(x + dx, 4)]
        copies.append(pltpu.make_async_copy(pieces[k].at[:, :, :, some], to, sems.at[k]))
    for h in range(2):
        to = held.at[h, :, lax.rem(x + 2, 4)]
        src = pieces[3 + h].at[0, :, :, some]
        copies.append(pltpu.make_async_copy(src, to, sems.at[3 + h]))
    return copies


def weights_of(held, n):
    return held[:, :, :, :, n].reshape(D, CH)


def start(copies):
    for copy in copies:
        copy.start()


def wait(copies):
    for copy in copies:
        copy.wait()


def recur_kernel(meta, *refs):
    pieces = (refs[0:5], refs[5:10])
    conv_w, bias, rates = refs[15:18]
    decays_out, states_out, ends = refs[18:21]
    feat, held, exts, decays, states, x_sems, w_sems, out_sems = refs[21:]
    w, x, q = meta[0], meta[4], meta[2] * 2 + meta[1]
    to_held = weight_copies(refs[10:15], 1, held, x, w_sems)
    groups = piece_copies(pieces, feat, x_sems, w)
    start(groups[0] + to_held)
    start(groups[1] + groups[2] + groups[3])
    chans = pl.ds(pl.multiple_of(q * CH, CH), CH)
    taps, biases, rate = conv_w[:, chans], bias[:, chans], rates[:, chans]

    def one(i):
        ext = exts.at[i % 2]
        ext[...] = dot(feat[i], weights_of(held, 0))
        conv = taps[0:1] * ext[HALO:]
        for k in range(1, KERNEL):
            conv = conv + taps[k : k + 1] * ext[HALO - k : HALO - k + STEPS]
        main = feat[i, HALO:]
        recur = jax.nn.sigmoid(dot(main, weights_of(held, 1)) + biases[0:1])
        inflow = jax.nn.sigmoid(dot(main, weights_of(held, 2)) + biases[1:2])
        decay = jnp.exp(-8.0 * recur * rate)
        drive = jnp.sqrt(1.0 - decay * decay) * inflow * conv
        for lane in range(LANES):
            cols = slice(lane * 128, (lane + 1) * 128)
            decays[lane, pl.ds(i, STEPS, stride=SEQS), :] = decay[:, cols]
            states[lane, pl.ds(i, STEPS, stride=SEQS), :] = drive[:, cols]

    wait(to_held)
    for n, group in enumerate(groups):
        wait(group)
        one(n * 2)
        one(n * 2 + 1)

    def step(t, carry):
        at = pl.ds(pl.multiple_of(t * SEQS, SEQS), SEQS)
        done = []
        for lane, (state, product) in enumerate(carry):
            decay = decays[lane, at]
            state = decay * state + states[lane, at]
            product = product * decay
            states[lane, at] = state
            decays[lane, at] = product
            done.append((state, product))
        return tuple(done)

    last = ((jnp.zeros((SEQS, 128), F32), jnp.ones((SEQS, 128), F32)),) * LANES
    to_out = []
    for k in range(4):
        last = lax.fori_loop(k * STEPS // 4, (k + 1) * STEPS // 4, step, last, unroll=8)
        at = pl.ds(k * STEPS * SEQS // 4, STEPS * SEQS // 4)
        moved = [
            pltpu.make_async_copy(src.at[:, at], to.at[:, at], out_sems.at[k * 2 + n])
            for n, (src, to) in enumerate(((decays, decays_out), (states, states_out)))
        ]
        start(moved)
        to_out += moved
    for lane, (state, product) in enumerate(last):
        for k in range(8):
            ends[k, 0, :, lane * 128 : (lane + 1) * 128] = product
            ends[k, 1, :, lane * 128 : (lane + 1) * 128] = state
    wait(to_out)


def gate_kernel(meta, *refs):
    pieces = (refs[0:5], refs[5:10])
    decays_in, states_in = refs[15:17]
    out = refs[18]
    feat, held, decays, states, both, x_sems, w_sems, in_sems, out_sems = refs[19:]
    w, x = meta[0], meta[4]
    to_held = weight_copies(refs[10:15], 0, held, x, w_sems)
    groups = piece_copies(pieces, feat, x_sems, w, HALO)
    to_in = [
        pltpu.make_async_copy(decays_in, decays, in_sems.at[0]),
        pltpu.make_async_copy(states_in, states, in_sems.at[1]),
    ]
    start(groups[0] + to_held + to_in)
    start(groups[1] + groups[2] + groups[3])

    def moved(i):
        return pltpu.make_async_copy(both.at[i], out.at[i], out_sems.at[i])

    def one(i):
        gated = jax.nn.gelu(dot(feat[i], weights_of(held, 0)))
        at = pl.ds(i, STEPS, stride=SEQS)
        for lane in range(LANES):
            cols = slice(lane * 128, (lane + 1) * 128)
            both[i, 0, :, cols] = decays[lane, at, :] * gated[:, cols]
            both[i, 1, :, cols] = states[lane, at, :] * gated[:, cols]
        moved(i).start()

    wait(to_held)
    for n, group in enumerate(groups):
        wait(group)
        if n == 0:
            wait(to_in)
        one(n * 2)
        one(n * 2 + 1)
    wait([moved(i) for i in range(SEQS)])


def mix_kernel(meta, gated, blocks, out, both, mixed, in_sems, out_sems):
    c, yh, z = meta[1], meta[2], meta[3]
    to_both = [
        pltpu.make_async_copy(gated.at[i], both.at[i], in_sems.at[i]) for i in range(SEQS)
    ]
    start(to_both)
    row = lax.broadcasted_iota(jnp.int32, (SEQS, CH), 0)
    late = jnp.where(row < 4, yh, 1 - yh) == 1
    whole = jnp.zeros((SEQS, CH), F32)
    for k in range(8):
        whole = blocks[k, 0] * whole + blocks[k, 1]
    incoming = jnp.where(late, pltpu.roll(whole, 4, 0), 0.0)
    for k in range(8):
        incoming = jnp.where(k < z, blocks[k, 0] * incoming + blocks[k, 1], incoming)
    to_out = []
    for i in range(SEQS):
        block, core, game = i // 4, (i // 2) % 2, i % 2
        yb = yh if block == 0 else 1 - yh
        cb = c if core == 0 else 1 - c
        to_both[i].wait()
        mixed[i] = (both[i, 1] + both[i, 0] * incoming[i : i + 1]).astype(BF16)
        to = out.at[(yb * 2 + cb) * 2 + game]
        to_out.append(pltpu.make_async_copy(mixed.at[i], to, out_sems.at[i]))
        to_out[i].start()
    wait(to_out)


def down_copies(pieces, down_w, w, c, yh, x, sems):
    column, beside, beside_c, across, across_c = pieces
    halves = ((across, 2, 4 * c), (across_c, 2, 4 - 4 * c))
    wholes = ((column, 0), (beside, 3 - 2 * c), (beside_c, 1 + 2 * c))
    groups = []
    for n, (h, rel) in enumerate(((yh, ((0, w), (1, 1 - w))), (1 - yh, ((3, w), (2, 1 - w))))):
        for part in range(2):
            copies = []
            for r, v in rel:
                at = pl.ds(pl.multiple_of(v * HALF, HALF), HALF)
                moved = [(src.at[part * 4 : part * 4 + 4, :, r], dx, part * 4) for src, dx in wholes]
                if part == 0:
                    moved += [(src.at[:, :, r], dx, first) for src, dx, first in halves]
                for src, dx, first in moved:
                    to = down_w.at[h, pl.ds(first, 4), lax.rem(x + dx, 4), :, :, at]
                    sem = sems.at[n * 2 + part, len(copies)]
                    copies.append(pltpu.make_async_copy(src, to, sem))
            groups.append(copies)
    return groups


def head_kernel(
    meta,
    lengths,
    outcomes,
    moves,
    own,
    pair,
    mixed,
    column,
    beside,
    beside_c,
    across,
    across_c,
    heads,
    heads_oth,
    out,
    feat,
    mix,
    down_w,
    resid,
    wp,
    f_sems,
    m_sems,
    d_sems,
):
    w, c, yh, z, x = meta[0], meta[1], meta[2], meta[3], meta[4]
    to_mix = []
    for j in range(SEQS):
        to = mix.at[:, pl.ds((j % 2) * HALF + (j // 2) * CH, CH)]
        to_mix.append(pltpu.make_async_copy(mixed.at[j], to, m_sems.at[j]))
    pieces = (column, beside, beside_c, across, across_c)
    to_down = down_copies(pieces, down_w, w, c, yh, x, d_sems)
    to_feat = [
        pltpu.make_async_copy(own.at[w], feat.at[w], f_sems.at[0]),
        pltpu.make_async_copy(pair.at[w], feat.at[1 - w], f_sems.at[1]),
    ]
    to_wp = [
        pltpu.make_async_copy(heads, wp.at[w], f_sems.at[2]),
        pltpu.make_async_copy(heads_oth, wp.at[1 - w], f_sems.at[3]),
    ]
    start(to_mix + to_down[0] + to_feat + to_down[1] + to_down[2] + to_down[3] + to_wp)
    wait(to_mix)
    square = jnp.zeros((STEPS, 1), F32)
    width = 512
    for k in range(4):
        h, j = (yh if k < 2 else 1 - yh), k % 2
        wait(to_down[k])
        rows = down_w[h, j * 4 : (j + 1) * 4].reshape(width, D)
        down = lax.dot_general(
            mix[...], rows, (((1,), (1,)), ((), ())), preferred_element_type=F32
        )
        if k == 0:
            wait(to_feat)
        at = slice(j * width, (j + 1) * width)
        value = (feat[h, HALO:, at].astype(F32) + down).astype(BF16)
        resid[h, :, at] = value
        wide = value.astype(F32)
        square = square + jnp.sum(wide * wide, axis=1, keepdims=True)
    wait(to_wp)
    raw = dot(resid[0], wp[0]) + dot(resid[1], wp[1])
    norm = lax.rsqrt(square / D + 1e-06)
    logits = raw * norm
    column = lax.broadcasted_iota(jnp.int32, logits.shape, 1)
    policy = column < MOVES
    top = jnp.max(jnp.where(policy, logits, -jnp.inf), axis=1, keepdims=True)
    total = jnp.sum(jnp.where(policy, jnp.exp(logits - top), 0.0), axis=1, keepdims=True)
    lse = top + jnp.log(total)
    played = jnp.broadcast_to(moves[pl.ds(w, 1), :].astype(F32), (128, STEPS)).T
    played = jnp.concatenate([played] * (COLS // 128), axis=1).astype(jnp.int32)
    picked = jnp.sum(jnp.where(column == played, logits, 0.0), axis=1, keepdims=True)
    score = jnp.sum(jnp.where(column == MOVES, logits, 0.0), axis=1, keepdims=True)
    value = jnp.tanh(score)
    place = (yh * 8 + z) * STEPS + lax.broadcasted_iota(jnp.int32, (STEPS, 1), 0)
    miss = value - outcomes[w].astype(F32)
    loss = jnp.where(place < lengths[w], lse - picked + miss * miss, 0.0)
    lane = lax.broadcasted_iota(jnp.int32, (STEPS, 128), 1)
    both = jnp.where(lane == 0, loss, jnp.where(lane == 1, value, 0.0))
    out[...] = both.T[0:2]


def params():
    return pltpu.CompilerParams(vmem_limit_bytes=VMEM_LIMIT)


def shards(
    moves,
    lengths,
    outcomes,
    embedded,
    w_branches,
    conv_w,
    gate_bias,
    rates,
    w_down,
    w_policy,
    w_value,
):
    yh, z, x, c, w = (lax.axis_index(a) for a in ("yh", "z", "x", "c", "w"))
    meta = jnp.stack([w, c, yh, z, x]).astype(jnp.int32)
    ring = ("yh", "w")
    together = lax.optimization_barrier

    halo = lax.ppermute(embedded[:, STEPS - HALO :], ("yh", "z"), [(k, k + 1) for k in range(15)])
    quarters = w_branches.reshape(4, 16, 2, 2, CH).transpose(2, 3, 0, 1, 4)
    quarters = jnp.broadcast_to(quarters[:, None], (2, 8, 2, 4, 16, CH)).reshape(32, 4, 16, CH)
    rows = lax.all_to_all(quarters, ("yh", "z", "c"), 0, 0, tiled=True)
    rows = rows.reshape(2, 8, 2, 4, 16, CH)
    parts = [w_down] + [lax.ppermute(w_down, ring, p) for p in (PAIR, OTHER, turn(4, 2))]
    halo, parts = together((halo, parts))

    own = jnp.concatenate([halo, embedded], axis=1)
    column = lax.all_gather(jnp.stack(parts), ("z", "c"), axis=0).reshape(8, 2, 4, 16, HALF)
    swap = lambda a: lax.ppermute(a, "c", SWAP)
    pair, other = lax.ppermute(own, ring, PAIR), lax.ppermute(own, ring, OTHER)
    behind, ahead = lax.ppermute(rows, "x", turn(4, 1)), lax.ppermute(rows, "x", turn(4, 3))
    own_c = swap(own)
    heads = jnp.concatenate(
        [w_policy, w_value[:, None], jnp.zeros((HALF, COLS - MOVES - 1), BF16)], axis=1
    )
    pair, other, behind, ahead, own_c, heads, pair_half, other_half, meta = together(
        (pair, other, behind, ahead, own_c, heads, pair[1], other[0], meta)
    )
    far0 = lax.ppermute(other_half, ring, PAIR)
    far1 = lax.ppermute(pair_half, ring, OTHER)
    low = lax.ppermute(behind[:1], "x", turn(4, 1))
    high = lax.ppermute(ahead[1:], "x", turn(4, 3))
    pair_c = swap(pair)
    far0, far1, low, high, pair_c, late, column = together(
        (far0, far1, low, high, pair_c, other, column)
    )
    apart = [(k, (k + 2 if k % 2 == 0 else k - 2) % 8) for k in range(8)]
    other_c, far0_c, far1_c = swap(late), swap(far0), swap(far1)
    beside = lax.ppermute(column, ("x", "c"), apart)
    mine = (own, pair, other, far0, far1)
    theirs = (own_c, pair_c, other_c, far0_c, far1_c)
    weights = (rows, behind, ahead, low, high)

    x_scratch = pltpu.VMEM((SEQS, ROWS, D), BF16)
    w_scratch = lambda n: pltpu.VMEM((2, 8, 4, 2, n, 16, CH), BF16)
    by_step = (LANES, STEPS * SEQS, 128)
    sems = lambda n: pltpu.SemaphoreType.DMA((n,))
    decays, states, ends = pl.pallas_call(
        recur_kernel,
        name="recur",
        out_shape=(
            jax.ShapeDtypeStruct(by_step, F32),
            jax.ShapeDtypeStruct(by_step, F32),
            jax.ShapeDtypeStruct((8, 2, SEQS, CH), F32),
        ),
        in_specs=[SM] + [ANY] * 15 + [VM] * 3,
        out_specs=(ANY, ANY, VM),
        scratch_shapes=[
            x_scratch,
            w_scratch(3),
            pltpu.VMEM((2, ROWS, CH), F32),
            pltpu.VMEM(by_step, F32),
            pltpu.VMEM(by_step, F32),
            sems(12),
            sems(5),
            sems(8),
        ],
        compiler_params=params(),
        cost_estimate=pl.CostEstimate(
            flops=2 * 2048 * 2048 * 768, bytes_accessed=15 << 20, transcendentals=5 << 19
        ),
    )(meta, *mine, *theirs, *weights, conv_w, gate_bias, rates[None])

    beside, _ = together((beside, ends))
    beside_c = swap(beside)
    across = lax.dynamic_slice_in_dim(beside, c * 4, 4, 0)
    across = lax.ppermute(across, ("x", "c"), apart)
    heads, _ = together((heads, far0))
    heads_oth = lax.ppermute(heads, "w", SWAP)
    blocks = lax.all_to_all(ends, "z", 0, 0, tiled=True)
    gated = pl.pallas_call(
        gate_kernel,
        name="gate",
        out_shape=jax.ShapeDtypeStruct((SEQS, 2, STEPS, CH), F32),
        in_specs=[SM] + [ANY] * 18,
        out_specs=ANY,
        scratch_shapes=[
            pltpu.VMEM((SEQS, STEPS, D), BF16),
            w_scratch(1),
            pltpu.VMEM(by_step, F32),
            pltpu.VMEM(by_step, F32),
            pltpu.VMEM((SEQS, 2, STEPS, CH), F32),
            sems(12),
            sems(5),
            sems(2),
            sems(8),
        ],
        compiler_params=params(),
        cost_estimate=pl.CostEstimate(
            flops=2 * 2048 * 2048 * 2048, bytes_accessed=60 << 20, transcendentals=1 << 19
        ),
    )(meta, *mine, *theirs, *weights, decays, states, heads_oth)

    mixed = pl.pallas_call(
        mix_kernel,
        name="mix",
        out_shape=jax.ShapeDtypeStruct((SEQS, STEPS, CH), BF16),
        in_specs=[SM, ANY, VM],
        out_specs=ANY,
        scratch_shapes=[
            pltpu.VMEM((SEQS, 2, STEPS, CH), F32),
            pltpu.VMEM((SEQS, STEPS, CH), BF16),
            sems(8),
            sems(8),
        ],
        compiler_params=params(),
        cost_estimate=pl.CostEstimate(flops=4 << 19, bytes_accessed=5 << 20, transcendentals=0),
    )(meta, gated, blocks)
    across, mixed = together((across, mixed))
    across_c = swap(across)
    mixed = lax.all_to_all(mixed, ("yh", "c", "w"), 0, 0, tiled=True)

    out = pl.pallas_call(
        head_kernel,
        name="head",
        out_shape=jax.ShapeDtypeStruct((2, STEPS), F32),
        in_specs=[SM, SM, SM, VM] + [ANY] * 10,
        out_specs=VM,
        scratch_shapes=[
            pltpu.VMEM((2, ROWS, HALF), BF16),
            pltpu.VMEM((STEPS, D), BF16),
            pltpu.VMEM((2, 8, 4, 2, 16, D), BF16),
            pltpu.VMEM((2, STEPS, HALF), BF16),
            pltpu.VMEM((2, HALF, COLS), BF16),
            sems(4),
            sems(8),
            pltpu.SemaphoreType.DMA((4, 10)),
        ],
        compiler_params=params(),
        cost_estimate=pl.CostEstimate(
            flops=2 * 256 * 2048 * 2432, bytes_accessed=12 << 20, transcendentals=1 << 17
        ),
    )(meta, lengths, outcomes, moves, own, pair, mixed, column, beside, beside_c, across, across_c, heads, heads_oth)
    here = out
    there = lax.ppermute(here, "w", SWAP)
    game = lax.broadcasted_iota(jnp.int32, (2, STEPS), 0) == w
    return (jnp.where(game, here[:1], there[:1]), jnp.where(game, here[1:], there[1:]))


def solution(mesh):
    fine = Mesh(mesh.devices.reshape(2, 8, 4, 2, 2), ("yh", "z", "x", "c", "w"))
    tm, batch = ("yh", "z"), ("x", "c")
    in_specs = (
        P(batch, tm),
        P(batch),
        P(batch),
        P(batch, tm, "w"),
        P(None, tm + batch, "w"),
        P(None, "w"),
        P(None, "w"),
        P("w"),
        P(tm + batch, "w"),
        P("w", None),
        P("w"),
    )
    out_specs = (P(batch, tm), P(batch, tm))
    return jax.shard_map(
        shards, mesh=fine, in_specs=in_specs, out_specs=out_specs, check_vma=False
    )
```
